32 devices in a mesh: rep: 2 (over x), shard: 16 (over z, y, core).
Axes of the slice: x: 2, y: 2, z: 4, core: 2. Of those that a mesh axis runs over, the one named last changes fastest.
Arguments:
- block_input: bfloat16 [4096, 2048], P(('rep', 'shard')), may hold values from -6 to 6
- out_grad: bfloat16 [4096, 2048], P(('rep', 'shard')), may hold values from -6 to 6
- segments: int32 [32, 128], P(('rep', 'shard')), may hold values from 0 to 2, as said below
- positions: int32 [32, 128], P(('rep', 'shard')), may hold values from 0 to 1023, as said below
- attn_gain: float32 [2048], replicated, may hold values from 0.5 to 1.5
- mlp_gain: float32 [2048], replicated, may hold values from 0.5 to 1.5
- q_gain: float32 [128], replicated, may hold values from 0.5 to 2
- k_gain: float32 [128], replicated, may hold values from 0.5 to 2
- w_q: bfloat16 [2048, 2048], P('shard'), may hold values from -0.125 to 0.125
- key_matrix: bfloat16 [2048, 1024], P('shard'), may hold values from -0.125 to 0.125
- value_matrix: bfloat16 [2048, 1024], P('shard'), may hold values from -0.125 to 0.125
- w_o: bfloat16 [2048, 2048], P('shard'), may hold values from -0.75 to 0.75
- w_gate: bfloat16 [2048, 6144], P('shard'), may hold values from -0.125 to 0.125
- w_up: bfloat16 [2048, 6144], P('shard'), may hold values from -0.125 to 0.125
- w_down: bfloat16 [2048, 6144], P('shard'), may hold values from -0.078125 to 0.078125
Outputs:
- output: bfloat16 [4096, 2048], P(('rep', 'shard'))
- grad_input: float32 [4096, 2048], P(('rep', 'shard'))
- grad_w_q: float32 [2048, 2048], P('shard')
- grad_w_k: float32 [2048, 1024], P('shard')
- grad_w_v: float32 [2048, 1024], P('shard')
- grad_w_o: float32 [2048, 2048], P('shard')
- grad_w_gate: float32 [2048, 6144], P('shard')
- grad_w_up: float32 [2048, 6144], P('shard')
- grad_w_down: float32 [2048, 6144], P('shard')
- grad_attn_gain: float32 [2048], replicated
- grad_mlp_gain: float32 [2048], replicated
- grad_q_gain: float32 [128], replicated
- grad_k_gain: float32 [128], replicated
The draws below stay inside these ranges and needn't reach their ends.
Inputs may be any that keep to these rules, and one draw needn't show every extreme that they name: `segments`: in each sequence the segment numbers never fall, the first token has 0 and the last has 2. Within a segment the positions rise by one from token to token; segments 1 and 2 start at position 0.
All inputs are finite; a program needn't handle non-finite values.
Results may differ from the reference program's by a relative error of at most 0.015.
Values may be sent and summed in bfloat16 or wider, within the bound.
No kernel may reach another device: no remote copies, remote signals or barrier semaphores. Data moves between devices by JAX's collectives and lax.ppermute only.
A program may use at most 768 MiB of HBM per device.

```python
import math
import jax
import jax.numpy as jnp
from jax import lax

MODEL_WIDTH = 2048
QUERY_HEADS = 16
KEY_VALUE_HEADS = 8
HEAD_SIZE = 128
FF = 6144
LEN = 128
SEQS = 32
TOKENS = 4096


def segment_layout(key):
    base = jax.random.fold_in(key, 11)
    cuts = jnp.sort(jax.random.randint(base, (SEQS, 2), 1, LEN), axis=1).astype(jnp.int32)
    places = jnp.arange(LEN, dtype=jnp.int32)[None, :]
    numbers = (places >= cuts[:, 0:1]).astype(jnp.int32) + (places >= cuts[:, 1:2]).astype(jnp.int32)
    first_cut = cuts[:, 0:1]
    drawn = jax.random.randint(jax.random.fold_in(base, 3), (SEQS, 1), 0, 1025 - first_cut).astype(jnp.int32)
    rows_index = jnp.arange(SEQS, dtype=jnp.int32)[:, None]
    offsets = jnp.where(rows_index == 0, 1024 - first_cut, drawn).astype(jnp.int32)
    begins = jnp.where(numbers == 0, -offsets, jnp.where(numbers == 1, cuts[:, 0:1], cuts[:, 1:2]))
    return (numbers, (places - begins).astype(jnp.int32))


def draw_segments(key, part):
    return segment_layout(key)[0]


def draw_positions(key, part):
    return segment_layout(key)[1]


def raised(array, stream_key, source, target, parts, factor):
    owner, partner = [(jnp.arange(array.shape[dim]) // (array.shape[dim] // parts)).reshape([-1 if axis == dim else 1 for axis in range(array.ndim)]) for dim in (source, target)]
    chosen = jax.random.permutation(stream_key, parts)[partner]
    strong = (owner == chosen) | (owner == (partner + parts // 2) % parts)
    return jnp.where(strong, factor * array, array)


def level_of(own_key, shape, shards, least, largest):
    def one(dim, blocks):
        draws = jax.random.uniform(jax.random.fold_in(jax.random.fold_in(own_key, 6), dim), (blocks,), jnp.float32, least / len(shards), largest / len(shards))
        return jnp.repeat(jnp.exp(draws), shape[dim] // blocks).reshape((-1,) + (1,) * (len(shape) - dim - 1))

    loudness = one(*shards[0])
    for cut in shards[1:]:
        loudness = loudness * one(*cut)
    return loudness


def centred(key, dims, deviation, most, shards=(), kind=jnp.bfloat16):
    factor_of = level_of(key, dims, shards, -0.22, 0.18) if shards else 1.0
    result = jax.random.normal(key, dims, jnp.float32) * deviation * factor_of
    return jnp.minimum(jnp.maximum(result, -most), most).astype(kind)


def heavy_noise(key, shape, width, limit, shards, heavy, kind=jnp.bfloat16):
    values = width * jax.random.normal(key, shape, jnp.float32)
    if shards:
        values = values * level_of(key, shape, shards, -0.22, 0.18)
    return jnp.clip(raised(values, jax.random.fold_in(key, 3), *heavy), -limit, limit).astype(kind)


def setup_inputs(seed: int = 0) -> dict:
    seeds = jax.random.split(jax.random.key(seed), 16)
    block_input = heavy_noise(seeds[0], (TOKENS, MODEL_WIDTH), 1.0, 6.0, ((0, 32),), (0, 1, 32, 2.75))
    out_grad = heavy_noise(seeds[1], (TOKENS, MODEL_WIDTH), 1.0, 6.0, ((0, 32),), (0, 1, 32, 2.75))
    segments = draw_segments(jax.random.fold_in(seeds[15], 71), 0)
    positions = draw_positions(jax.random.fold_in(seeds[15], 71), 0)
    attn_gain = jnp.clip(1.0 + 0.1 * jax.random.normal(seeds[4], (MODEL_WIDTH,), jnp.float32), 0.5, 1.5)
    mlp_gain = jnp.clip(1.0 + 0.1 * jax.random.normal(seeds[5], (MODEL_WIDTH,), jnp.float32), 0.5, 1.5)
    q_gain = jnp.clip(jnp.exp(jax.random.uniform(seeds[6], (HEAD_SIZE,), jnp.float32, math.log(0.5), math.log(2.0))), 0.5, 2.0)
    k_gain = jnp.clip(jnp.exp(jax.random.uniform(seeds[7], (HEAD_SIZE,), jnp.float32, math.log(0.5), math.log(2.0))), 0.5, 2.0)
    w_q = centred(seeds[8], (MODEL_WIDTH, QUERY_HEADS * HEAD_SIZE), MODEL_WIDTH ** -0.5, 0.125, ((0, 16),))
    key_matrix = centred(seeds[9], (MODEL_WIDTH, KEY_VALUE_HEADS * HEAD_SIZE), MODEL_WIDTH ** -0.5, 0.125, ((0, 16),))
    value_matrix = centred(seeds[10], (MODEL_WIDTH, KEY_VALUE_HEADS * HEAD_SIZE), MODEL_WIDTH ** -0.5, 0.125, ((0, 16),))
    w_o = centred(seeds[11], (MODEL_WIDTH, QUERY_HEADS * HEAD_SIZE), (QUERY_HEADS * HEAD_SIZE // 32) ** -0.5, 0.75, ((0, 16),))
    w_gate = centred(seeds[12], (MODEL_WIDTH, FF), MODEL_WIDTH ** -0.5, 0.125, ((0, 16),))
    w_up = centred(seeds[13], (MODEL_WIDTH, FF), MODEL_WIDTH ** -0.5, 0.125, ((0, 16),))
    w_down = centred(seeds[14], (MODEL_WIDTH, FF), FF ** -0.5, 0.078125, ((0, 16),))
    return dict(block_input=block_input, out_grad=out_grad, segments=segments, positions=positions, attn_gain=attn_gain, mlp_gain=mlp_gain, q_gain=q_gain, k_gain=k_gain, w_q=w_q, key_matrix=key_matrix, value_matrix=value_matrix, w_o=w_o, w_gate=w_gate, w_up=w_up, w_down=w_down)


EPSILON = 1e-06
ROPE_BASE = 1000000.0
NEG_FILL = -1e+30

def rope_tables(positions, half):
    freq = jnp.exp(jnp.arange(half, dtype=jnp.float32) * (-math.log(ROPE_BASE) / half))
    angles = positions.reshape(-1).astype(jnp.float32)[:, None, None] * freq
    return (jnp.cos(angles), jnp.sin(angles))

def rotate(vectors, cosine, sine):
    half = vectors.shape[-1] // 2
    first, second = (vectors[..., :half], vectors[..., half:])
    return jnp.concatenate([first * cosine - second * sine, second * cosine + first * sine], -1)

def unrotate(grads, cosine, sine):
    half = grads.shape[-1] // 2
    first, second = (grads[..., :half], grads[..., half:])
    return jnp.concatenate([first * cosine + second * sine, second * cosine - first * sine], -1)

def head_norm(heads, gain):
    recip = lax.rsqrt(lax.optimization_barrier(jnp.mean(heads * heads, -1, keepdims=True)) + EPSILON)
    return (heads * recip * gain, recip)

def norm_back(grads, inputs, recip, gain, axes):
    normal = inputs * recip
    scaled = grads * gain
    gain_grad = lax.optimization_barrier(jnp.sum(grads * normal, axis=axes))
    input_grad = recip * (scaled - normal * lax.optimization_barrier(jnp.mean(scaled * normal, -1, keepdims=True)))
    return (input_grad, gain_grad)

def attention_mask(segments):
    packed_length = segments.shape[1]
    same = segments[:, :, None] == segments[:, None, :]
    places = jnp.arange(packed_length)
    causal = places[None, :] <= places[:, None]
    return same & causal[None]

def head_scores(rotated_query_rows, rotated_key_rows, mask):
    sequence_list, packed_length = (mask.shape[0], mask.shape[1])
    query_rows = rotated_query_rows.astype(jnp.float32).reshape(sequence_list, packed_length, KEY_VALUE_HEADS, QUERY_HEADS // KEY_VALUE_HEADS, HEAD_SIZE)
    every_key_row = rotated_key_rows.astype(jnp.float32).reshape(sequence_list, packed_length, KEY_VALUE_HEADS, HEAD_SIZE)
    scores = jnp.einsum('slkgd,smkd->skglm', query_rows, every_key_row) * HEAD_SIZE ** (-0.5)
    return (jnp.where(mask[:, None, None], scores, NEG_FILL), query_rows, every_key_row)

def attend_forward(rotated_query_rows, rotated_key_rows, value_rows, mask):
    sequence_list, packed_length = (mask.shape[0], mask.shape[1])
    scores, query_rows, every_key_row = head_scores(rotated_query_rows, rotated_key_rows, mask)
    top = lax.optimization_barrier(jnp.max(scores, -1, keepdims=True))
    expo = jnp.exp(scores - top)
    total = lax.optimization_barrier(jnp.sum(expo, -1, keepdims=True))
    probs = (expo / total).astype(jnp.bfloat16)
    log_total = top + jnp.log(total)
    value_heads = value_rows.astype(jnp.float32).reshape(sequence_list, packed_length, KEY_VALUE_HEADS, HEAD_SIZE)
    attended_rows = jnp.einsum('skglm,smkd->slkgd', probs.astype(jnp.float32), value_heads)
    return (attended_rows.reshape(sequence_list * packed_length, QUERY_HEADS * HEAD_SIZE).astype(jnp.bfloat16), log_total)

def attend_backward(rotated_query_rows, rotated_key_rows, value_rows, attended_rows, attended_gradient, log_total, mask):
    sequence_list, packed_length = (mask.shape[0], mask.shape[1])
    scores, query_rows, every_key_row = head_scores(rotated_query_rows, rotated_key_rows, mask)
    probs_back = jnp.where(mask[:, None, None], jnp.exp(scores - log_total), 0.0)
    probs_b = probs_back.astype(jnp.bfloat16).astype(jnp.float32)
    output_gradient = attended_gradient.astype(jnp.float32).reshape(sequence_list, packed_length, KEY_VALUE_HEADS, QUERY_HEADS // KEY_VALUE_HEADS, HEAD_SIZE)
    complete_output = attended_rows.astype(jnp.float32).reshape(sequence_list, packed_length, KEY_VALUE_HEADS, QUERY_HEADS // KEY_VALUE_HEADS, HEAD_SIZE)
    value_heads = value_rows.astype(jnp.float32).reshape(sequence_list, packed_length, KEY_VALUE_HEADS, HEAD_SIZE)
    value_rows_gradient = jnp.einsum('skglm,slkgd->smkd', probs_b, output_gradient)
    grad_probs = jnp.einsum('slkgd,smkd->skglm', output_gradient, value_heads)
    delta = jnp.transpose(lax.optimization_barrier(jnp.sum(output_gradient * complete_output, -1)), (0, 2, 3, 1))[..., None]
    grad_scores = (probs_back * (grad_probs - delta)).astype(jnp.bfloat16).astype(jnp.float32)
    rotated_query_gradient = jnp.einsum('skglm,smkd->slkgd', grad_scores, every_key_row) * HEAD_SIZE ** (-0.5)
    rotated_key_gradient = jnp.einsum('skglm,slkgd->smkd', grad_scores, query_rows) * HEAD_SIZE ** (-0.5)
    token_rows = sequence_list * packed_length
    return (rotated_query_gradient.reshape(token_rows, QUERY_HEADS, HEAD_SIZE), rotated_key_gradient.reshape(token_rows, KEY_VALUE_HEADS, HEAD_SIZE), value_rows_gradient.reshape(token_rows, KEY_VALUE_HEADS, HEAD_SIZE))

def layer_pass(block_input, out_grad, segments, positions, gains, weights):
    attn_gain, mlp_gain, q_gain, k_gain = gains
    w_q, key_matrix, value_matrix, w_o, w_gate, w_up, w_down = weights
    token_rows = block_input.shape[0]
    mask = attention_mask(segments)
    cosine, sine = rope_tables(positions, HEAD_SIZE // 2)
    inputs = block_input.astype(jnp.float32)
    recip_attn = lax.rsqrt(lax.optimization_barrier(jnp.mean(inputs * inputs, -1, keepdims=True)) + EPSILON)
    normed_rows = (inputs * recip_attn * attn_gain).astype(jnp.bfloat16)
    q_heads = jnp.dot(normed_rows, w_q, preferred_element_type=jnp.float32).reshape(token_rows, QUERY_HEADS, HEAD_SIZE)
    key_head_rows = jnp.dot(normed_rows, key_matrix, preferred_element_type=jnp.float32).reshape(token_rows, KEY_VALUE_HEADS, HEAD_SIZE)
    value_rows = jnp.dot(normed_rows, value_matrix, preferred_element_type=jnp.float32).astype(jnp.bfloat16)
    q_normed, q_recip = head_norm(q_heads, q_gain)
    k_normed, k_recip = head_norm(key_head_rows, k_gain)
    rotated_query_rows = rotate(q_normed, cosine, sine).astype(jnp.bfloat16)
    rotated_key_rows = rotate(k_normed, cosine, sine).astype(jnp.bfloat16)
    attended_rows, log_total = attend_forward(rotated_query_rows, rotated_key_rows, value_rows, mask)
    mid = inputs + jnp.dot(attended_rows, w_o.T, preferred_element_type=jnp.float32)
    recip_mlp = lax.rsqrt(lax.optimization_barrier(jnp.mean(mid * mid, -1, keepdims=True)) + EPSILON)
    mlp_in = (mid * recip_mlp * mlp_gain).astype(jnp.bfloat16)
    gate_pre = jnp.dot(mlp_in, w_gate, preferred_element_type=jnp.float32)
    up_pre = jnp.dot(mlp_in, w_up, preferred_element_type=jnp.float32)
    sigma = jax.nn.sigmoid(gate_pre)
    silu_gate = gate_pre * sigma
    act = (silu_gate * up_pre).astype(jnp.bfloat16)
    output = (mid + jnp.dot(act, w_down.T, preferred_element_type=jnp.float32)).astype(jnp.bfloat16)
    grad_top = out_grad.astype(jnp.float32)
    grad_act = jnp.dot(out_grad, w_down, preferred_element_type=jnp.float32)
    grad_gate = (grad_act * up_pre * sigma * (1.0 + gate_pre * (1.0 - sigma))).astype(jnp.bfloat16)
    grad_up = (grad_act * silu_gate).astype(jnp.bfloat16)
    grad_w_gate = jnp.dot(mlp_in.T, grad_gate, preferred_element_type=jnp.float32)
    grad_w_up = jnp.dot(mlp_in.T, grad_up, preferred_element_type=jnp.float32)
    grad_w_down = jnp.dot(out_grad.T, act, preferred_element_type=jnp.float32)
    grad_mlp_in = jnp.dot(grad_gate, w_gate.T, preferred_element_type=jnp.float32) + jnp.dot(grad_up, w_up.T, preferred_element_type=jnp.float32)
    grad_mid_part, grad_mlp_gain = norm_back(grad_mlp_in, mid, recip_mlp, mlp_gain, 0)
    grad_mid = grad_top + grad_mid_part
    grad_mid_b = grad_mid.astype(jnp.bfloat16)
    grad_w_o = jnp.dot(grad_mid_b.T, attended_rows, preferred_element_type=jnp.float32)
    attended_gradient = jnp.dot(grad_mid_b, w_o, preferred_element_type=jnp.float32).astype(jnp.bfloat16)
    rotated_query_gradient, rotated_key_gradient, value_rows_gradient = attend_backward(rotated_query_rows, rotated_key_rows, value_rows, attended_rows, attended_gradient, log_total, mask)
    grad_qh, grad_q_gain = norm_back(unrotate(rotated_query_gradient, cosine, sine), q_heads, q_recip, q_gain, (0, 1))
    key_heads_gradient, grad_k_gain = norm_back(unrotate(rotated_key_gradient, cosine, sine), key_head_rows, k_recip, k_gain, (0, 1))
    grad_q = grad_qh.reshape(token_rows, QUERY_HEADS * HEAD_SIZE).astype(jnp.bfloat16)
    key_gradient = key_heads_gradient.reshape(token_rows, KEY_VALUE_HEADS * HEAD_SIZE).astype(jnp.bfloat16)
    value_gradient = value_rows_gradient.reshape(token_rows, KEY_VALUE_HEADS * HEAD_SIZE).astype(jnp.bfloat16)
    grad_w_q = jnp.dot(normed_rows.T, grad_q, preferred_element_type=jnp.float32)
    grad_w_k = jnp.dot(normed_rows.T, key_gradient, preferred_element_type=jnp.float32)
    grad_w_v = jnp.dot(normed_rows.T, value_gradient, preferred_element_type=jnp.float32)
    grad_normed = jnp.dot(grad_q, w_q.T, preferred_element_type=jnp.float32) + jnp.dot(key_gradient, key_matrix.T, preferred_element_type=jnp.float32) + jnp.dot(value_gradient, value_matrix.T, preferred_element_type=jnp.float32)
    grad_in_part, grad_attn_gain = norm_back(grad_normed, inputs, recip_attn, attn_gain, 0)
    grad_input = grad_mid + grad_in_part
    weight_grads = (grad_w_q, grad_w_k, grad_w_v, grad_w_o, grad_w_gate, grad_w_up, grad_w_down)
    gain_grads = (grad_attn_gain, grad_mlp_gain, grad_q_gain, grad_k_gain)
    return (output, grad_input, weight_grads, gain_grads)

def reference(block_input, out_grad, segments, positions, attn_gain, mlp_gain, q_gain, k_gain, w_q, key_matrix, value_matrix, w_o, w_gate, w_up, w_down):
    block_seqs = math.gcd(SEQS, max(1, 4096 // LEN))
    blocks = SEQS // block_seqs
    token_rows = block_seqs * LEN
    gains = (attn_gain, mlp_gain, q_gain, k_gain)
    weights = (w_q, key_matrix, value_matrix, w_o, w_gate, w_up, w_down)
    inputs_blocks = block_input.reshape(blocks, token_rows, MODEL_WIDTH)
    grads_blocks = out_grad.reshape(blocks, token_rows, MODEL_WIDTH)
    seg_blocks = segments.reshape(blocks, block_seqs, LEN)
    pos_blocks = positions.reshape(blocks, block_seqs, LEN)
    init_weights = tuple((jnp.zeros(w.shape, jnp.float32) for w in weights))
    init_gains = tuple((jnp.zeros(g.shape, jnp.float32) for g in gains))

    def scan_step(running, pieces):
        output, grad_input, weight_grads, gain_grads = layer_pass(pieces[0], pieces[1], pieces[2], pieces[3], gains, weights)
        sums_w = jax.tree.map(lambda left, right: left + right, running[0], weight_grads)
        sums_g = jax.tree.map(lambda left, right: left + right, running[1], gain_grads)
        return ((sums_w, sums_g), (output, grad_input))
    totals, stacked = lax.scan(scan_step, (init_weights, init_gains), (inputs_blocks, grads_blocks, seg_blocks, pos_blocks))
    weight_sums, gain_sums = totals
    return (stacked[0].reshape(TOKENS, MODEL_WIDTH), stacked[1].reshape(TOKENS, MODEL_WIDTH), weight_sums[0], weight_sums[1], weight_sums[2], weight_sums[3], weight_sums[4], weight_sums[5], weight_sums[6], gain_sums[0], gain_sums[1], gain_sums[2], gain_sums[3])
```

```python
import math

import jax
import jax.numpy as jnp
from jax import lax
from jax.sharding import Mesh
from jax.sharding import PartitionSpec as P

EPSILON = 1e-06
ROPE_BASE = 1000000.0
NEG_FILL = -1e30
F32 = jnp.float32
BF16 = jnp.bfloat16
SWAP = [(0, 1), (1, 0)]
CHUNK = 2048


def over_rep(v):
    return lax.ppermute(v, "rep", SWAP)


def over_mid(v):
    return lax.ppermute(v, "mid", SWAP)


def over_near(v):
    return lax.ppermute(v, "near", SWAP)


def plane_gather(own):
    half = own.shape[0] // 2
    from_rep = over_rep(own)
    from_mid = over_mid(own)
    top = over_mid(from_rep[:half])
    bottom = over_rep(from_mid[half:])
    mine = jnp.concatenate([own, from_rep, from_mid, top, bottom], 0)
    return jnp.concatenate([mine, over_near(mine)], 0)


def plane_scatter(left, contract):
    middle = left.shape[0] // 2
    rows = middle // 4
    half = rows // 2
    near = over_near(contract(left[middle:]).astype(BF16))
    part = contract(left[:middle]) + near.astype(F32)
    own, rep, mid, both = (part[i * rows : (i + 1) * rows] for i in range(4))
    first_rep = over_rep(jnp.concatenate([both[:half], rep[:half]], 0).astype(BF16))
    first_mid = over_mid(jnp.concatenate([both[half:], mid[half:]], 0).astype(BF16))
    last_mid = over_mid((mid[:half] + first_rep[:half].astype(F32)).astype(BF16))
    last_rep = over_rep((rep[half:] + first_mid[:half].astype(F32)).astype(BF16))
    top = own[:half] + first_rep[half:].astype(F32) + last_mid.astype(F32)
    bottom = own[half:] + last_rep.astype(F32) + first_mid[half:].astype(F32)
    return jnp.concatenate([top, bottom], 0)


def line_gather(block, size):
    m, rows, n = block.shape
    if size > 4:
        return lax.all_gather(block, "far", axis=1, tiled=True)
    place = lax.axis_index("far")
    right, left = [block], [block]
    for k in range(1, size):
        right.append(lax.ppermute(right[-1], "far", [(i, i + 1) for i in range(k - 1, size - 1)]))
        left.append(lax.ppermute(left[-1], "far", [(i, i - 1) for i in range(1, size - k + 1)]))
    out = jnp.zeros((m, size * rows, n), block.dtype)
    out = lax.dynamic_update_slice(out, block, (0, place * rows, 0))
    for k in range(1, size):
        piece = jnp.where(place >= k, right[k], left[size - k])
        out = lax.dynamic_update_slice(out, piece, (0, (place - k) % size * rows, 0))
    return out


def line_scatter(parts, size):
    m, full, n = parts.shape
    rows = full // size
    if size > 4:
        return lax.psum_scatter(parts, "far", scatter_dimension=1, tiled=True)
    place = lax.axis_index("far")

    def block(index):
        return lax.dynamic_slice(parts, (0, index % size * rows, 0), (m, rows, n))

    right = left = None
    for k in range(size - 1, 0, -1):
        onward, back = block(place + k), block(place - k)
        if right is not None:
            onward = (onward.astype(F32) + right.astype(F32)).astype(parts.dtype)
            back = (back.astype(F32) + left.astype(F32)).astype(parts.dtype)
        right = lax.ppermute(onward, "far", [(i, i + 1) for i in range(0, size - k)])
        left = lax.ppermute(back, "far", [(i, i - 1) for i in range(k, size)])
    out = block(place).astype(F32)
    if right is not None:
        out = out + right.astype(F32) + left.astype(F32)
    return out.astype(parts.dtype)


def fetch_columns(pieces, size):
    side = lax.axis_index("rep")
    stacked = jnp.stack([p.reshape(p.shape[0], 2, 4, -1) for p in pieces])
    mine = lax.dynamic_index_in_dim(stacked, side, 2, keepdims=False)
    ready = jnp.transpose(mine, (2, 0, 1, 3))
    swapped = lax.all_to_all(ready, ("mid", "near"), 0, 0)
    m, rows, n = mine.shape[0], mine.shape[1], mine.shape[3]
    block = jnp.transpose(swapped, (1, 0, 2, 3)).reshape(m, 4 * rows, n)
    return line_gather(block, size)


def return_rows(grads, size):
    mine = line_scatter(grads, size)
    m, four, n = mine.shape
    rows = four // 4
    ready = jnp.transpose(mine.reshape(m, 4, rows, n), (1, 0, 2, 3))
    swapped = lax.all_to_all(ready, ("mid", "near"), 0, 0)
    other = over_rep(swapped)
    side = lax.axis_index("rep")
    low = jnp.where(side == 0, swapped, other)
    high = jnp.where(side == 0, other, swapped)
    both = jnp.stack([low, high])
    return jnp.transpose(both, (2, 3, 0, 1, 4)).reshape(m, rows, 8 * n).astype(F32)


def sum_everywhere(v, size):
    for axis in ("near", "mid", "rep"):
        v = v + lax.ppermute(v, axis, SWAP)
    if size & (size - 1):
        return lax.psum(v, "far")
    step = 1
    while step < size:
        v = v + lax.ppermute(v, "far", [(i, i ^ step) for i in range(size)])
        step *= 2
    return v


def rope_tables(positions, half):
    freq = jnp.exp(jnp.arange(half, dtype=F32) * (-math.log(ROPE_BASE) / half))
    angles = positions.reshape(-1).astype(F32)[:, None, None] * freq
    return (jnp.cos(angles), jnp.sin(angles))


def rotate(vectors, cosine, sine):
    half = vectors.shape[-1] // 2
    first, second = (vectors[..., :half], vectors[..., half:])
    return jnp.concatenate([first * cosine - second * sine, second * cosine + first * sine], -1)


def unrotate(grads, cosine, sine):
    half = grads.shape[-1] // 2
    first, second = (grads[..., :half], grads[..., half:])
    return jnp.concatenate([first * cosine + second * sine, second * cosine - first * sine], -1)


def head_norm(heads, gain):
    recip = lax.rsqrt(jnp.mean(heads * heads, -1, keepdims=True) + EPSILON)
    return (heads * recip * gain, recip)


def norm_back(grads, inputs, recip, gain, axes):
    normal = inputs * recip
    scaled = grads * gain
    gain_grad = jnp.sum(grads * normal, axis=axes)
    input_grad = recip * (scaled - normal * jnp.mean(scaled * normal, -1, keepdims=True))
    return (input_grad, gain_grad)


def attention_mask(segments):
    packed_length = segments.shape[1]
    same = segments[:, :, None] == segments[:, None, :]
    places = jnp.arange(packed_length)
    causal = places[None, :] <= places[:, None]
    return same & causal[None]


def dot(left, right):
    return jnp.dot(left, right, preferred_element_type=F32)


def contract_rows(left, right):
    return lax.dot_general(left, right, (((0,), (0,)), ((), ())), preferred_element_type=F32)


def contract_cols(left, right):
    return lax.dot_general(left, right, (((1,), (1,)), ((), ())), preferred_element_type=F32)


def head_scores(rotated_query_rows, rotated_key_rows, mask):
    sequences, length = (mask.shape[0], mask.shape[1])
    kv_heads, head = rotated_key_rows.shape[1:]
    groups = rotated_query_rows.shape[1] // kv_heads
    query_rows = rotated_query_rows.reshape(sequences, length, kv_heads, groups, head)
    key_rows = rotated_key_rows.reshape(sequences, length, kv_heads, head)
    scores = jnp.einsum("slkgd,smkd->skglm", query_rows, key_rows, preferred_element_type=F32) * head ** (-0.5)
    return (jnp.where(mask[:, None, None], scores, NEG_FILL), query_rows, key_rows)


def attend_forward(rotated_query_rows, rotated_key_rows, value_rows, mask):
    sequences, length = (mask.shape[0], mask.shape[1])
    kv_heads, head = (value_rows.shape[1], value_rows.shape[2])
    scores, _, _ = head_scores(rotated_query_rows, rotated_key_rows, mask)
    top = jnp.max(scores, -1, keepdims=True)
    expo = jnp.exp(scores - top)
    total = jnp.sum(expo, -1, keepdims=True)
    probs = (expo / total).astype(BF16)
    log_total = top + jnp.log(total)
    value_heads = value_rows.reshape(sequences, length, kv_heads, head)
    attended = jnp.einsum("skglm,smkd->slkgd", probs, value_heads, preferred_element_type=F32)
    return (attended.reshape(sequences * length, -1).astype(BF16), log_total)


def attend_backward(rotated_query_rows, rotated_key_rows, value_rows, attended_rows, attended_gradient, log_total, mask):
    sequences, length = (mask.shape[0], mask.shape[1])
    kv_heads, head = (value_rows.shape[1], value_rows.shape[2])
    groups = rotated_query_rows.shape[1] // kv_heads
    scores, query_rows, key_rows = head_scores(rotated_query_rows, rotated_key_rows, mask)
    probs_back = jnp.where(mask[:, None, None], jnp.exp(scores - log_total), 0.0)
    output_gradient = attended_gradient.reshape(sequences, length, kv_heads, groups, head)
    value_heads = value_rows.reshape(sequences, length, kv_heads, head)
    value_gradient = jnp.einsum(
        "skglm,slkgd->smkd", probs_back.astype(BF16), output_gradient, preferred_element_type=F32
    )
    grad_probs = jnp.einsum("slkgd,smkd->skglm", output_gradient, value_heads, preferred_element_type=F32)
    complete = attended_rows.reshape(sequences, length, kv_heads, groups, head).astype(F32)
    delta = jnp.transpose(jnp.sum(output_gradient.astype(F32) * complete, -1), (0, 2, 3, 1))[..., None]
    grad_scores = (probs_back * (grad_probs - delta)).astype(BF16)
    query_gradient = jnp.einsum("skglm,smkd->slkgd", grad_scores, key_rows, preferred_element_type=F32)
    key_gradient = jnp.einsum("skglm,slkgd->smkd", grad_scores, query_rows, preferred_element_type=F32)
    tokens = sequences * length
    return (
        query_gradient.reshape(tokens, kv_heads * groups, head) * head ** (-0.5),
        key_gradient.reshape(tokens, kv_heads, head) * head ** (-0.5),
        value_gradient.reshape(tokens, kv_heads, head),
    )


def gather_inputs(normed_rows, segments, positions):
    tokens, width = normed_rows.shape
    digits = jnp.concatenate(
        [segments >> 7, segments & 127, positions >> 7, positions & 127], 0
    ).astype(BF16)
    note = jnp.zeros((16, width), BF16).at[:4, : digits.shape[1]].set(digits)
    half = tokens // 2
    sent = jnp.concatenate([normed_rows[:half], note, normed_rows[half:], note], 0)
    every = plane_gather(sent).reshape(8, 2, half + 16, width)
    rows = every[:, :, :half].reshape(8 * tokens, width)
    notes = every[:, 0, half : half + 4, : digits.shape[1]].astype(jnp.int32)
    return (rows, notes[:, 0] * 128 + notes[:, 1], notes[:, 2] * 128 + notes[:, 3])


def build(far):
    def on_device(
        block_input,
        out_grad,
        segments,
        positions,
        attn_gain,
        mlp_gain,
        q_gain,
        k_gain,
        w_q,
        key_matrix,
        value_matrix,
        w_o,
        w_gate,
        w_up,
        w_down,
    ):
        head = q_gain.shape[0]
        heads = w_q.shape[1] // head // 8
        kv_heads = key_matrix.shape[1] // head // 8
        hidden = w_gate.shape[1]
        rows = w_q.shape[0]
        inputs = block_input.astype(F32)
        recip_attn = lax.rsqrt(jnp.mean(inputs * inputs, -1, keepdims=True) + EPSILON)
        normed_own = (inputs * recip_attn * attn_gain).astype(BF16)
        normed_rows, every_segment, every_position = gather_inputs(normed_own, segments, positions)
        tokens = normed_rows.shape[0]
        mask = attention_mask(every_segment)
        cosine, sine = rope_tables(every_position, head // 2)

        qkv_own = jnp.concatenate(
            [w.reshape(rows, 8, -1) for w in (w_q, key_matrix, value_matrix)], 2
        ).reshape(rows, -1)
        qkv = fetch_columns([qkv_own], far)[0]
        w_o_cols = fetch_columns([w_o], far)[0]
        q_cols = heads * head
        k_cols = kv_heads * head
        proj = dot(normed_rows, qkv)
        q_heads = proj[:, :q_cols].reshape(tokens, heads, head)
        key_head_rows = proj[:, q_cols : q_cols + k_cols].reshape(tokens, kv_heads, head)
        value_rows = proj[:, q_cols + k_cols :].astype(BF16).reshape(tokens, kv_heads, head)
        q_normed, q_recip = head_norm(q_heads, q_gain)
        k_normed, k_recip = head_norm(key_head_rows, k_gain)
        rotated_query_rows = rotate(q_normed, cosine, sine).astype(BF16)
        rotated_key_rows = rotate(k_normed, cosine, sine).astype(BF16)
        attended_rows, log_total = attend_forward(rotated_query_rows, rotated_key_rows, value_rows, mask)
        mid = inputs + plane_scatter(attended_rows, lambda left: contract_cols(left, w_o_cols))
        recip_mlp = lax.rsqrt(jnp.mean(mid * mid, -1, keepdims=True) + EPSILON)
        mlp_in = plane_gather((mid * recip_mlp * mlp_gain).astype(BF16))
        grad_top = plane_gather(out_grad)

        chunks = range(hidden // CHUNK)
        acts, downs, sides, side_weights, mlp_grads = [], [], [], [], []
        for j in chunks:
            span = slice(j * CHUNK, (j + 1) * CHUNK)
            three = fetch_columns([w_gate[:, span], w_up[:, span], w_down[:, span]], far)
            gate_pre = dot(mlp_in, three[0])
            up_pre = dot(mlp_in, three[1])
            sigma = jax.nn.sigmoid(gate_pre)
            silu_gate = gate_pre * sigma
            act = (silu_gate * up_pre).astype(BF16)
            grad_act = dot(grad_top, three[2])
            grad_gate = (grad_act * up_pre * sigma * (1.0 + gate_pre * (1.0 - sigma))).astype(BF16)
            grad_up = (grad_act * silu_gate).astype(BF16)
            own = jnp.stack(
                [
                    contract_rows(mlp_in, grad_gate).astype(BF16),
                    contract_rows(mlp_in, grad_up).astype(BF16),
                    contract_rows(grad_top, act).astype(BF16),
                ]
            )
            mlp_grads.append(return_rows(own, far))
            acts.append(act)
            downs.append(three[2])
            sides += [grad_gate, grad_up]
            side_weights += [three[0], three[1]]
        down = jnp.concatenate(downs, 1)
        sideways = jnp.concatenate(side_weights, 1)
        grad_mlp_in = plane_scatter(jnp.concatenate(sides, 1), lambda left: contract_cols(left, sideways))
        mlp_out = plane_scatter(jnp.concatenate(acts, 1), lambda left: contract_cols(left, down))
        output = (mid + mlp_out).astype(BF16)
        grad_mid_part, mlp_gain_part = norm_back(grad_mlp_in, mid, recip_mlp, mlp_gain, 0)
        grad_mid = out_grad.astype(F32) + grad_mid_part
        grad_mid_b = plane_gather(grad_mid.astype(BF16))
        attended_gradient = dot(grad_mid_b, w_o_cols).astype(BF16)
        own_o = contract_rows(grad_mid_b, attended_rows).astype(BF16)
        grad_w_o = return_rows(own_o[None], far)[0]
        query_gradient, key_gradient, value_gradient = attend_backward(
            rotated_query_rows,
            rotated_key_rows,
            value_rows,
            attended_rows,
            attended_gradient,
            log_total,
            mask,
        )
        grad_qh, q_gain_part = norm_back(unrotate(query_gradient, cosine, sine), q_heads, q_recip, q_gain, (0, 1))
        grad_kh, k_gain_part = norm_back(
            unrotate(key_gradient, cosine, sine), key_head_rows, k_recip, k_gain, (0, 1)
        )
        grad_qkv = jnp.concatenate(
            [g.reshape(tokens, -1).astype(BF16) for g in (grad_qh, grad_kh, value_gradient)], 1
        )
        own_qkv = contract_rows(normed_rows, grad_qkv).astype(BF16)
        every_qkv = return_rows(own_qkv[None], far)[0].reshape(rows, 8, -1)
        grad_normed = plane_scatter(grad_qkv, lambda left: contract_cols(left, qkv))
        grad_in_part, attn_gain_part = norm_back(grad_normed, inputs, recip_attn, attn_gain, 0)
        grad_input = grad_mid + grad_in_part
        width = inputs.shape[1]
        sums = sum_everywhere(
            jnp.concatenate([attn_gain_part, mlp_gain_part, q_gain_part, k_gain_part]).reshape(1, -1), far
        )[0]
        grad_gate_w, grad_up_w, grad_down_w = (
            jnp.concatenate([g[i] for g in mlp_grads], 1) for i in range(3)
        )
        return (
            output,
            grad_input,
            every_qkv[:, :, :q_cols].reshape(rows, -1),
            every_qkv[:, :, q_cols : q_cols + k_cols].reshape(rows, -1),
            every_qkv[:, :, q_cols + k_cols :].reshape(rows, -1),
            grad_w_o,
            grad_gate_w,
            grad_up_w,
            grad_down_w,
            sums[:width],
            sums[width : 2 * width],
            sums[2 * width : 2 * width + head],
            sums[2 * width + head :],
        )

    return on_device


def solution(mesh):
    far = mesh.shape["shard"] // 4
    split = Mesh(mesh.devices.reshape(mesh.shape["rep"], far, 2, 2), ("rep", "far", "mid", "near"))
    tokens = P(("rep", "far", "mid", "near"), None)
    weights = P(("far", "mid", "near"), None)
    return jax.shard_map(
        build(far),
        mesh=split,
        in_specs=(tokens,) * 4 + (P(),) * 4 + (weights,) * 7,
        out_specs=(tokens,) * 2 + (weights,) * 7 + (P(),) * 4,
        check_vma=False,
    )
```

```python
import math

import jax
import jax.numpy as jnp
from jax import lax
from jax.experimental import pallas as pl
from jax.experimental.pallas import tpu as pltpu
from jax.sharding import Mesh
from jax.sharding import PartitionSpec as P

EPSILON = 1e-06
ROPE_BASE = 1000000.0
NEG_FILL = -1e30
F32 = jnp.float32
BF16 = jnp.bfloat16
SWAP = [(0, 1), (1, 0)]
CHUNK = 2048


def over_rep(v):
    return lax.ppermute(v, "rep", SWAP)


def over_mid(v):
    return lax.ppermute(v, "mid", SWAP)


def over_near(v):
    return lax.ppermute(v, "near", SWAP)


def plane_gather(own):
    half = own.shape[0] // 2
    from_rep = over_rep(own)
    from_mid = over_mid(own)
    top = over_mid(from_rep[:half])
    bottom = over_rep(from_mid[half:])
    mine = jnp.concatenate([own, from_rep, from_mid, top, bottom], 0)
    return jnp.concatenate([mine, over_near(mine)], 0)


def plane_scatter(partial, rows):
    half = rows // 2
    near = over_near(partial(4 * rows, 8 * rows).astype(BF16))
    part = partial(0, 4 * rows) + near.astype(F32)
    own, rep, mid, both = (part[i * rows : (i + 1) * rows] for i in range(4))
    first_rep = over_rep(jnp.concatenate([both[:half], rep[:half]], 0).astype(BF16))
    first_mid = over_mid(jnp.concatenate([both[half:], mid[half:]], 0).astype(BF16))
    last_mid = over_mid((mid[:half] + first_rep[:half].astype(F32)).astype(BF16))
    last_rep = over_rep((rep[half:] + first_mid[:half].astype(F32)).astype(BF16))
    top = own[:half] + first_rep[half:].astype(F32) + last_mid.astype(F32)
    bottom = own[half:] + last_rep.astype(F32) + first_mid[half:].astype(F32)
    return jnp.concatenate([top, bottom], 0)


def pick_columns(groups):
    side = lax.axis_index("rep").astype(jnp.int32).reshape(1)
    members = [m for group in groups for m in group]
    rows = members[0][0].shape[0]
    widths = [sum(n for _, _, n in group) for group in groups]

    def kernel(side_ref, *refs):
        sources = iter(refs[: len(members)])
        for group, out in zip(groups, refs[len(members) :]):
            at = 0
            for _, _, n in group:
                source = next(sources)
                for block in range(4):
                    out[block, :, at : at + n] = source[:, block * n : (block + 1) * n]
                at += n

    def half(start, n):
        return pl.BlockSpec((rows, 4 * n), lambda i, side_ref: (0, start // (4 * n) + side_ref[0]))

    return pl.pallas_call(
        kernel,
        grid_spec=pltpu.PrefetchScalarGridSpec(
            num_scalar_prefetch=1,
            grid=(1,),
            in_specs=[half(start, n) for _, start, n in members],
            out_specs=[pl.BlockSpec((4, rows, w), lambda i, side_ref: (0, 0, 0)) for w in widths],
        ),
        out_shape=[jax.ShapeDtypeStruct((4, rows, w), BF16) for w in widths],
        name="pick_columns",
    )(side, *[m for m, _, _ in members])


def trade(blocks):
    return lax.all_to_all(blocks, ("mid", "near"), 0, 0)


def gather_rows(blocks):
    four, rows, n = blocks.shape
    return lax.all_gather(blocks.reshape(four * rows, n), "far", axis=0, tiled=True)


def scatter_rows(parts):
    mine = lax.psum_scatter(parts, "far", scatter_dimension=0, tiled=True)
    mine = trade(mine.reshape(4, mine.shape[0] // 4, -1))
    return (mine, over_rep(mine))


def spread(pairs, outs):
    side = lax.axis_index("rep").astype(jnp.int32).reshape(1)
    rows = pairs[0][0].shape[1]
    columns = [sum(8 * n for _, _, n in pieces) for pieces in outs]

    def kernel(side_ref, *refs):
        first = side_ref[0] == 0
        for out, pieces in zip(refs[2 * len(pairs) :], outs):
            at = 0
            for pair, start, n in pieces:
                own, other = refs[2 * pair], refs[2 * pair + 1]
                for block in range(4):
                    a = own[block, :, start : start + n].astype(F32)
                    b = other[block, :, start : start + n].astype(F32)
                    out[:, at + block * n : at + (block + 1) * n] = jnp.where(first, a, b)
                    out[:, at + (4 + block) * n : at + (5 + block) * n] = jnp.where(first, b, a)
                at += 8 * n

    return pl.pallas_call(
        kernel,
        in_specs=[pl.BlockSpec(memory_space=pltpu.SMEM)] + [pl.BlockSpec(memory_space=pltpu.VMEM)] * (2 * len(pairs)),
        out_specs=[pl.BlockSpec(memory_space=pltpu.VMEM)] * len(outs),
        out_shape=[jax.ShapeDtypeStruct((rows, c), F32) for c in columns],
        compiler_params=pltpu.CompilerParams(vmem_limit_bytes=40 << 20),
        name="spread",
    )(side, *[v for pair in pairs for v in pair])


def sum_everywhere(v, size):
    for axis in ("near", "mid", "rep"):
        v = v + lax.ppermute(v, axis, SWAP)
    if size & (size - 1):
        return lax.psum(v, "far")
    step = 1
    while step < size:
        v = v + lax.ppermute(v, "far", [(i, i ^ step) for i in range(size)])
        step *= 2
    return v


def rope_tables(positions, half):
    freq = jnp.exp(jnp.arange(half, dtype=F32) * (-math.log(ROPE_BASE) / half))
    angles = positions.reshape(-1).astype(F32)[:, None, None] * freq
    return (jnp.cos(angles), jnp.sin(angles))


def rotate(vectors, cosine, sine):
    half = vectors.shape[-1] // 2
    first, second = (vectors[..., :half], vectors[..., half:])
    return jnp.concatenate([first * cosine - second * sine, second * cosine + first * sine], -1)


def unrotate(grads, cosine, sine):
    half = grads.shape[-1] // 2
    first, second = (grads[..., :half], grads[..., half:])
    return jnp.concatenate([first * cosine + second * sine, second * cosine - first * sine], -1)


def head_norm(heads, gain):
    recip = lax.rsqrt(jnp.mean(heads * heads, -1, keepdims=True) + EPSILON)
    return (heads * recip * gain, recip)


def norm_back(grads, inputs, recip, gain, axes):
    normal = inputs * recip
    scaled = grads * gain
    gain_grad = jnp.sum(grads * normal, axis=axes)
    input_grad = recip * (scaled - normal * jnp.mean(scaled * normal, -1, keepdims=True))
    return (input_grad, gain_grad)


def attention_mask(segments):
    packed_length = segments.shape[1]
    same = segments[:, :, None] == segments[:, None, :]
    places = jnp.arange(packed_length)
    causal = places[None, :] <= places[:, None]
    return same & causal[None]


def dot(left, right):
    return jnp.dot(left, right, preferred_element_type=F32)


def contract_rows(left, right):
    return lax.dot_general(left, right, (((0,), (0,)), ((), ())), preferred_element_type=F32)


def contract_cols(left, right):
    return lax.dot_general(left, right, (((1,), (1,)), ((), ())), preferred_element_type=F32)


def head_scores(rotated_query_rows, rotated_key_rows, mask):
    sequences, length = (mask.shape[0], mask.shape[1])
    kv_heads, head = rotated_key_rows.shape[1:]
    groups = rotated_query_rows.shape[1] // kv_heads
    query_rows = rotated_query_rows.reshape(sequences, length, kv_heads, groups, head)
    key_rows = rotated_key_rows.reshape(sequences, length, kv_heads, head)
    scores = jnp.einsum("slkgd,smkd->skglm", query_rows, key_rows, preferred_element_type=F32) * head ** (-0.5)
    return (jnp.where(mask[:, None, None], scores, NEG_FILL), query_rows, key_rows)


def attend_forward(rotated_query_rows, rotated_key_rows, value_rows, mask):
    sequences, length = (mask.shape[0], mask.shape[1])
    kv_heads, head = (value_rows.shape[1], value_rows.shape[2])
    scores, _, _ = head_scores(rotated_query_rows, rotated_key_rows, mask)
    top = jnp.max(scores, -1, keepdims=True)
    expo = jnp.exp(scores - top)
    total = jnp.sum(expo, -1, keepdims=True)
    probs = (expo / total).astype(BF16)
    log_total = top + jnp.log(total)
    value_heads = value_rows.reshape(sequences, length, kv_heads, head)
    attended = jnp.einsum("skglm,smkd->slkgd", probs, value_heads, preferred_element_type=F32)
    return (attended.reshape(sequences * length, -1).astype(BF16), log_total)


def attend_backward(rotated_query_rows, rotated_key_rows, value_rows, attended_rows, attended_gradient, log_total, mask):
    sequences, length = (mask.shape[0], mask.shape[1])
    kv_heads, head = (value_rows.shape[1], value_rows.shape[2])
    groups = rotated_query_rows.shape[1] // kv_heads
    scores, query_rows, key_rows = head_scores(rotated_query_rows, rotated_key_rows, mask)
    probs_back = jnp.where(mask[:, None, None], jnp.exp(scores - log_total), 0.0)
    output_gradient = attended_gradient.reshape(sequences, length, kv_heads, groups, head)
    value_heads = value_rows.reshape(sequences, length, kv_heads, head)
    value_gradient = jnp.einsum(
        "skglm,slkgd->smkd", probs_back.astype(BF16), output_gradient, preferred_element_type=F32
    )
    grad_probs = jnp.einsum("slkgd,smkd->skglm", output_gradient, value_heads, preferred_element_type=F32)
    complete = attended_rows.reshape(sequences, length, kv_heads, groups, head).astype(F32)
    delta = jnp.transpose(jnp.sum(output_gradient.astype(F32) * complete, -1), (0, 2, 3, 1))[..., None]
    grad_scores = (probs_back * (grad_probs - delta)).astype(BF16)
    query_gradient = jnp.einsum("skglm,smkd->slkgd", grad_scores, key_rows, preferred_element_type=F32)
    key_gradient = jnp.einsum("skglm,slkgd->smkd", grad_scores, query_rows, preferred_element_type=F32)
    tokens = sequences * length
    return (
        query_gradient.reshape(tokens, kv_heads * groups, head) * head ** (-0.5),
        key_gradient.reshape(tokens, kv_heads, head) * head ** (-0.5),
        value_gradient.reshape(tokens, kv_heads, head),
    )


def plane_notes(own):
    pair = jnp.concatenate([own, over_near(own)], 0)
    four = jnp.concatenate([pair, over_mid(pair)], 0)
    eight = jnp.concatenate([four, over_rep(four)], 0)
    return jnp.concatenate([eight[i : i + 1] for i in (0, 4, 2, 6, 1, 5, 3, 7)], 0)


def build(far):
    def on_device(
        block_input,
        out_grad,
        segments,
        positions,
        attn_gain,
        mlp_gain,
        q_gain,
        k_gain,
        w_q,
        key_matrix,
        value_matrix,
        w_o,
        w_gate,
        w_up,
        w_down,
    ):
        head = q_gain.shape[0]
        heads = w_q.shape[1] // head // 8
        kv_heads = key_matrix.shape[1] // head // 8
        hidden = w_gate.shape[1]
        rows = w_q.shape[0]
        q_cols = heads * head
        k_cols = kv_heads * head
        chunks = list(range(0, hidden, CHUNK))

        q_n, k_n, o_n, block = (n // 8 for n in (w_q.shape[1], key_matrix.shape[1], w_o.shape[1], CHUNK))
        qkv_slot, o_slot = pick_columns(
            [[(w_q, 0, q_n), (key_matrix, 0, k_n), (value_matrix, 0, k_n)], [(w_o, 0, o_n)]]
        )
        qkv = gather_rows(trade(qkv_slot))
        w_o_cols = gather_rows(trade(o_slot))
        mlp_slots = pick_columns([[(w, c, block) for w in (w_gate, w_up, w_down)] for c in chunks])
        mlp_weights = [gather_rows(trade(slot)) for slot in mlp_slots]

        inputs = block_input.astype(F32)
        recip_attn = lax.rsqrt(jnp.mean(inputs * inputs, -1, keepdims=True) + EPSILON)
        normed_rows = plane_gather((inputs * recip_attn * attn_gain).astype(BF16))
        grad_top = plane_gather(out_grad)
        notes = plane_notes(jnp.concatenate([segments, positions], 1))
        length = segments.shape[1]
        own_tokens = inputs.shape[0]
        tokens = normed_rows.shape[0]
        mask = attention_mask(notes[:, :length])
        cosine, sine = rope_tables(notes[:, length:], head // 2)

        proj = dot(normed_rows, qkv)
        q_heads = proj[:, :q_cols].reshape(tokens, heads, head)
        key_head_rows = proj[:, q_cols : q_cols + k_cols].reshape(tokens, kv_heads, head)
        value_rows = proj[:, q_cols + k_cols :].astype(BF16).reshape(tokens, kv_heads, head)
        q_normed, q_recip = head_norm(q_heads, q_gain)
        k_normed, k_recip = head_norm(key_head_rows, k_gain)
        rotated_query_rows = rotate(q_normed, cosine, sine).astype(BF16)
        rotated_key_rows = rotate(k_normed, cosine, sine).astype(BF16)
        attended_rows, log_total = attend_forward(rotated_query_rows, rotated_key_rows, value_rows, mask)
        attended_rows, grad_top = lax.optimization_barrier((attended_rows, grad_top))
        mid = inputs + plane_scatter(lambda i, j: contract_cols(attended_rows[i:j], w_o_cols), own_tokens)
        recip_mlp = lax.rsqrt(jnp.mean(mid * mid, -1, keepdims=True) + EPSILON)
        mlp_in = plane_gather((mid * recip_mlp * mlp_gain).astype(BF16))

        acts, downs, mlp_grads = [], [], []
        before = None
        for number, three in enumerate(mlp_weights):
            weight = three[:, : 2 * block]
            pre = dot(mlp_in, weight)
            gate_pre, up_pre = pre[:, :block], pre[:, block:]
            sigma = jax.nn.sigmoid(gate_pre)
            silu_gate = gate_pre * sigma
            act = (silu_gate * up_pre).astype(BF16)
            grad_act = dot(grad_top, three[:, 2 * block :])
            grad_gate = (grad_act * up_pre * sigma * (1.0 + gate_pre * (1.0 - sigma))).astype(BF16)
            grad_up = (grad_act * silu_gate).astype(BF16)
            both = jnp.concatenate([grad_gate, grad_up], 1)
            own = jnp.concatenate([contract_rows(mlp_in, both), contract_rows(grad_top, act)], 1).astype(BF16)
            mlp_grads.append(scatter_rows(own))
            acts.append(act)
            downs.append(three[:, 2 * block :])
            if number < len(mlp_weights) - 1:
                part = contract_cols(both, weight)
                before = part if before is None else before + part
        grad_mlp_in = plane_scatter(
            lambda i, j: contract_cols(both[i:j], weight) + (0.0 if before is None else before[i:j]), own_tokens
        )
        grad_mid_part, mlp_gain_part = norm_back(grad_mlp_in, mid, recip_mlp, mlp_gain, 0)
        grad_mid = out_grad.astype(F32) + grad_mid_part
        grad_mid_b = plane_gather(grad_mid.astype(BF16))
        act = jnp.concatenate(acts, 1)
        act, grad_mid_b = lax.optimization_barrier((act, grad_mid_b))
        down = jnp.concatenate(downs, 1)
        mlp_out = plane_scatter(lambda i, j: contract_cols(act[i:j], down), own_tokens)
        output = (mid + mlp_out).astype(BF16)
        attended_gradient = dot(grad_mid_b, w_o_cols).astype(BF16)
        own_o = contract_rows(grad_mid_b, attended_rows).astype(BF16)
        o_pair = scatter_rows(own_o)
        query_gradient, key_gradient, value_gradient = attend_backward(
            rotated_query_rows,
            rotated_key_rows,
            value_rows,
            attended_rows,
            attended_gradient,
            log_total,
            mask,
        )
        grad_qh, q_gain_part = norm_back(unrotate(query_gradient, cosine, sine), q_heads, q_recip, q_gain, (0, 1))
        grad_kh, k_gain_part = norm_back(
            unrotate(key_gradient, cosine, sine), key_head_rows, k_recip, k_gain, (0, 1)
        )
        grad_qkv = jnp.concatenate(
            [g.reshape(tokens, -1).astype(BF16) for g in (grad_qh, grad_kh, value_gradient)], 1
        )
        own_qkv = contract_rows(normed_rows, grad_qkv).astype(BF16)
        qkv_pair = scatter_rows(own_qkv)
        grad_normed = plane_scatter(lambda i, j: contract_cols(grad_qkv[i:j], qkv), own_tokens)
        grad_in_part, attn_gain_part = norm_back(grad_normed, inputs, recip_attn, attn_gain, 0)
        grad_input = grad_mid + grad_in_part
        width = inputs.shape[1]
        sums = sum_everywhere(
            jnp.concatenate([attn_gain_part, mlp_gain_part, q_gain_part, k_gain_part]).reshape(1, -1), far
        )[0]
        by_chunk = range(len(chunks))
        grad_w_gate, grad_w_up, grad_w_down = spread(
            mlp_grads, [[(j, m * block, block) for j in by_chunk] for m in range(3)]
        )
        grad_w_q, grad_w_k, grad_w_v, grad_w_o = spread(
            [qkv_pair, o_pair], [[(0, 0, q_n)], [(0, q_n, k_n)], [(0, q_n + k_n, k_n)], [(1, 0, o_n)]]
        )
        return (
            output,
            grad_input,
            grad_w_q,
            grad_w_k,
            grad_w_v,
            grad_w_o,
            grad_w_gate,
            grad_w_up,
            grad_w_down,
            sums[:width],
            sums[width : 2 * width],
            sums[2 * width : 2 * width + head],
            sums[2 * width + head :],
        )

    return on_device


def solution(mesh):
    far = mesh.shape["shard"] // 4
    split = Mesh(mesh.devices.reshape(mesh.shape["rep"], far, 2, 2), ("rep", "far", "mid", "near"))
    tokens = P(("rep", "far", "mid", "near"), None)
    weights = P(("far", "mid", "near"), None)
    return jax.shard_map(
        build(far),
        mesh=split,
        in_specs=(tokens,) * 4 + (P(),) * 4 + (weights,) * 7,
        out_specs=(tokens,) * 2 + (weights,) * 7 + (P(),) * 4,
        check_vma=False,
    )
```

```python
import math

import jax
import jax.numpy as jnp
from jax import lax
from jax.experimental import pallas as pl
from jax.experimental.pallas import tpu as pltpu
from jax.sharding import Mesh
from jax.sharding import PartitionSpec as P

EPSILON = 1e-06
ROPE_BASE = 1000000.0
NEG_FILL = -1e30
F32 = jnp.float32
BF16 = jnp.bfloat16
SWAP = [(0, 1), (1, 0)]


def over_rep(v):
    return lax.ppermute(v, "rep", SWAP)


def over_mid(v):
    return lax.ppermute(v, "mid", SWAP)


def over_near(v):
    return lax.ppermute(v, "near", SWAP)


def plane_gather(own):
    half = own.shape[0] // 2
    from_rep = over_rep(own)
    from_mid = over_mid(own)
    top = over_mid(from_rep[:half])
    bottom = over_rep(from_mid[half:])
    mine = jnp.concatenate([own, from_rep, from_mid, top, bottom], 0)
    return jnp.concatenate([mine, over_near(mine)], 0)


def plane_scatter(partial, rows):
    half = rows // 2
    near = over_near(partial(4 * rows, 8 * rows).astype(BF16))
    part = partial(0, 4 * rows) + near.astype(F32)
    own, rep, mid, both = (part[i * rows : (i + 1) * rows] for i in range(4))
    first_rep = over_rep(jnp.concatenate([both[:half], rep[:half]], 0).astype(BF16))
    first_mid = over_mid(jnp.concatenate([both[half:], mid[half:]], 0).astype(BF16))
    last_mid = over_mid((mid[:half] + first_rep[:half].astype(F32)).astype(BF16))
    last_rep = over_rep((rep[half:] + first_mid[:half].astype(F32)).astype(BF16))
    top = own[:half] + first_rep[half:].astype(F32) + last_mid.astype(F32)
    bottom = own[half:] + last_rep.astype(F32) + first_mid[half:].astype(F32)
    return jnp.concatenate([top, bottom], 0)


def pick_columns(groups):
    side = lax.axis_index("rep").astype(jnp.int32).reshape(1)
    members = [m for group in groups for m in group]
    rows = members[0][0].shape[0]
    widths = [sum(n for _, _, n in group) for group in groups]

    def kernel(side_ref, *refs):
        sources = iter(refs[: len(members)])
        for group, out in zip(groups, refs[len(members) :]):
            at = 0
            for _, _, n in group:
                source = next(sources)
                for block in range(4):
                    out[block, :, at : at + n] = source[:, block * n : (block + 1) * n]
                at += n

    def half(start, n):
        return pl.BlockSpec((rows, 4 * n), lambda i, side_ref: (0, start // (4 * n) + side_ref[0]))

    return pl.pallas_call(
        kernel,
        grid_spec=pltpu.PrefetchScalarGridSpec(
            num_scalar_prefetch=1,
            grid=(1,),
            in_specs=[half(start, n) for _, start, n in members],
            out_specs=[pl.BlockSpec((4, rows, w), lambda i, side_ref: (0, 0, 0)) for w in widths],
        ),
        out_shape=[jax.ShapeDtypeStruct((4, rows, w), BF16) for w in widths],
        compiler_params=pltpu.CompilerParams(vmem_limit_bytes=20 << 20),
        name="pick_columns",
    )(side, *[m for m, _, _ in members])


def trade(blocks):
    return lax.all_to_all(blocks, ("mid", "near"), 0, 0)


def gather_rows(blocks):
    four, rows, n = blocks.shape
    return lax.all_gather(blocks.reshape(four * rows, n), "far", axis=0, tiled=True)


def queue_scatter(parts):
    return lax.psum_scatter(parts, "far", scatter_dimension=0, tiled=True)


def hand_out(mine):
    mine = trade(mine.reshape(4, mine.shape[0] // 4, -1))
    return (mine, over_rep(mine))


def spread(pairs, outs):
    side = lax.axis_index("rep").astype(jnp.int32).reshape(1)
    rows = pairs[0][0].shape[1]
    columns = [sum(8 * n for _, _, n in pieces) for pieces in outs]

    def kernel(side_ref, *refs):
        first = side_ref[0] == 0
        for out, pieces in zip(refs[2 * len(pairs) :], outs):
            at = 0
            for pair, start, n in pieces:
                own, other = refs[2 * pair], refs[2 * pair + 1]
                for block in range(4):
                    a = own[block, :, start : start + n].astype(F32)
                    b = other[block, :, start : start + n].astype(F32)
                    out[:, at + block * n : at + (block + 1) * n] = jnp.where(first, a, b)
                    out[:, at + (4 + block) * n : at + (5 + block) * n] = jnp.where(first, b, a)
                at += 8 * n

    return pl.pallas_call(
        kernel,
        in_specs=[pl.BlockSpec(memory_space=pltpu.SMEM)] + [pl.BlockSpec(memory_space=pltpu.VMEM)] * (2 * len(pairs)),
        out_specs=[pl.BlockSpec(memory_space=pltpu.VMEM)] * len(outs),
        out_shape=[jax.ShapeDtypeStruct((rows, c), F32) for c in columns],
        compiler_params=pltpu.CompilerParams(vmem_limit_bytes=40 << 20),
        name="spread",
    )(side, *[v for pair in pairs for v in pair])


def sum_everywhere(v, size):
    for axis in ("near", "mid", "rep"):
        v = v + lax.ppermute(v, axis, SWAP)
    if size & (size - 1):
        return lax.psum(v, "far")
    step = 1
    while step < size:
        v = v + lax.ppermute(v, "far", [(i, i ^ step) for i in range(size)])
        step *= 2
    return v


def after(*values):
    return lax.optimization_barrier(values)


def rope_tables(positions, half):
    freq = jnp.exp(jnp.arange(half, dtype=F32) * (-math.log(ROPE_BASE) / half))
    angles = positions.reshape(-1).astype(F32)[:, None] * freq
    cosine, sine = (jnp.cos(angles), jnp.sin(angles))
    return (jnp.concatenate([cosine, cosine], 1), jnp.concatenate([-sine, sine], 1))


def norm_back(grads, inputs, recip, gain, axes):
    normal = inputs * recip
    scaled = grads * gain
    gain_grad = jnp.sum(grads * normal, axis=axes)
    input_grad = recip * (scaled - normal * jnp.mean(scaled * normal, -1, keepdims=True))
    return (input_grad, gain_grad)


def dot(left, right):
    return jnp.dot(left, right, preferred_element_type=F32)


def contract_rows(left, right):
    return lax.dot_general(left, right, (((0,), (0,)), ((), ())), preferred_element_type=F32)


def contract_cols(left, right):
    return lax.dot_general(left, right, (((1,), (1,)), ((), ())), preferred_element_type=F32)


def swap_halves(v):
    half = v.shape[-1] // 2
    return jnp.concatenate([v[:, half:], v[:, :half]], -1)


def unit(u):
    recip = lax.rsqrt(jnp.mean(u * u, -1, keepdims=True) + EPSILON)
    return (u * recip, recip)


def sequence_state(proj_ref, cosine_ref, sine_ref, down_ref, across_ref, head):
    length = proj_ref.shape[0]
    later = lax.broadcasted_iota(jnp.int32, (length, length), 0)
    earlier = lax.broadcasted_iota(jnp.int32, (length, length), 1)
    mask = (down_ref[...] == across_ref[0]) & (earlier <= later)
    cosine, sine = cosine_ref[...], sine_ref[...]

    def turned(v):
        return v * cosine + swap_halves(v) * sine

    def turned_back(v):
        return v * cosine - swap_halves(v) * sine

    def columns(i):
        return proj_ref[:, i * head : (i + 1) * head]

    return (mask, turned, turned_back, columns)


def masked_scores(query, key, mask, head):
    return jnp.where(mask, contract_cols(query, key) * head ** (-0.5), NEG_FILL)


def attention_forward(proj, cosine, sine, down, across, q_gain, k_gain, heads, kv_heads):
    head = q_gain.shape[1]
    sequences, _, length = across.shape
    groups = heads // kv_heads

    def kernel(proj_ref, cosine_ref, sine_ref, down_ref, across_ref, q_gain_ref, k_gain_ref, out_ref):
        mask, turned, _, columns = sequence_state(proj_ref, cosine_ref, sine_ref, down_ref, across_ref, head)
        for kv in range(kv_heads):
            key = turned(unit(columns(heads + kv))[0] * k_gain_ref[...]).astype(BF16)
            value = columns(heads + kv_heads + kv).astype(BF16)
            for h in range(kv * groups, (kv + 1) * groups):
                query = turned(unit(columns(h))[0] * q_gain_ref[...]).astype(BF16)
                scores = masked_scores(query, key, mask, head)
                expo = jnp.exp(scores - jnp.max(scores, -1, keepdims=True))
                probs = (expo / jnp.sum(expo, -1, keepdims=True)).astype(BF16)
                out_ref[:, h * head : (h + 1) * head] = dot(probs, value).astype(BF16)

    row = lambda n: pl.BlockSpec((length, n), lambda i: (i, 0))
    fixed = pl.BlockSpec((1, head), lambda i: (0, 0))
    return pl.pallas_call(
        kernel,
        grid=(sequences,),
        in_specs=[row(proj.shape[1]), row(head), row(head), row(1)]
        + [pl.BlockSpec((1, 1, length), lambda i: (i, 0, 0)), fixed, fixed],
        out_specs=row(heads * head),
        out_shape=jax.ShapeDtypeStruct((proj.shape[0], heads * head), BF16),
        compiler_params=pltpu.CompilerParams(vmem_limit_bytes=6 << 20),
        name="attention_forward",
    )(proj, cosine, sine, down, across, q_gain, k_gain)


def attention_backward(proj, cosine, sine, down, across, q_gain, k_gain, attended, attended_grad, heads, kv_heads):
    head = q_gain.shape[1]
    sequences, _, length = across.shape
    groups = heads // kv_heads
    scale = head ** (-0.5)

    def kernel(
        proj_ref,
        cosine_ref,
        sine_ref,
        down_ref,
        across_ref,
        q_gain_ref,
        k_gain_ref,
        attended_ref,
        grad_ref,
        out_ref,
        gains_ref,
    ):
        mask, turned, turned_back, columns = sequence_state(
            proj_ref, cosine_ref, sine_ref, down_ref, across_ref, head
        )

        @pl.when(pl.program_id(0) == 0)
        def _():
            gains_ref[...] = jnp.zeros_like(gains_ref)

        def put(i, v):
            out_ref[:, i * head : (i + 1) * head] = v.astype(BF16)

        def norm_grad(i, grads, normal, recip, gain, row):
            scaled = grads * gain
            gains_ref[row : row + 1, :] += jnp.sum(grads * normal, 0, keepdims=True)
            put(i, recip * (scaled - normal * jnp.mean(scaled * normal, -1, keepdims=True)))

        for kv in range(kv_heads):
            key_unit, key_recip = unit(columns(heads + kv))
            key = turned(key_unit * k_gain_ref[...]).astype(BF16)
            value = columns(heads + kv_heads + kv).astype(BF16)
            grad_value = jnp.zeros((length, head), F32)
            grad_key = jnp.zeros((length, head), F32)
            for h in range(kv * groups, (kv + 1) * groups):
                query_unit, query_recip = unit(columns(h))
                query = turned(query_unit * q_gain_ref[...]).astype(BF16)
                scores = masked_scores(query, key, mask, head)
                top = jnp.max(scores, -1, keepdims=True)
                log_total = top + jnp.log(jnp.sum(jnp.exp(scores - top), -1, keepdims=True))
                probs = jnp.where(mask, jnp.exp(scores - log_total), 0.0)
                grad = grad_ref[:, h * head : (h + 1) * head]
                grad_value += contract_rows(probs.astype(BF16), grad)
                complete = attended_ref[:, h * head : (h + 1) * head].astype(F32)
                delta = jnp.sum(grad.astype(F32) * complete, -1, keepdims=True)
                grad_scores = (probs * (contract_cols(grad, value) - delta)).astype(BF16)
                grad_query = dot(grad_scores, key) * scale
                grad_key += contract_rows(grad_scores, query)
                norm_grad(h, turned_back(grad_query), query_unit, query_recip, q_gain_ref[...], 0)
            norm_grad(heads + kv, turned_back(grad_key * scale), key_unit, key_recip, k_gain_ref[...], 1)
            put(heads + kv_heads + kv, grad_value)

    row = lambda n: pl.BlockSpec((length, n), lambda i: (i, 0))
    fixed = pl.BlockSpec((1, head), lambda i: (0, 0))
    return pl.pallas_call(
        kernel,
        grid=(sequences,),
        in_specs=[row(proj.shape[1]), row(head), row(head), row(1)]
        + [pl.BlockSpec((1, 1, length), lambda i: (i, 0, 0)), fixed, fixed]
        + [row(heads * head), row(heads * head)],
        out_specs=[row(proj.shape[1]), pl.BlockSpec((8, head), lambda i: (0, 0))],
        out_shape=[jax.ShapeDtypeStruct(proj.shape, BF16), jax.ShapeDtypeStruct((8, head), F32)],
        compiler_params=pltpu.CompilerParams(vmem_limit_bytes=8 << 20),
        name="attention_backward",
    )(proj, cosine, sine, down, across, q_gain, k_gain, attended, attended_grad)


def plane_notes(own):
    pair = jnp.concatenate([own, over_near(own)], 0)
    four = jnp.concatenate([pair, over_mid(pair)], 0)
    eight = jnp.concatenate([four, over_rep(four)], 0)
    return jnp.concatenate([eight[i : i + 1] for i in (0, 4, 2, 6, 1, 5, 3, 7)], 0)


def build(far):
    def on_device(
        block_input,
        out_grad,
        segments,
        positions,
        attn_gain,
        mlp_gain,
        q_gain,
        k_gain,
        w_q,
        key_matrix,
        value_matrix,
        w_o,
        w_gate,
        w_up,
        w_down,
    ):
        head = q_gain.shape[0]
        heads = w_q.shape[1] // head // 8
        kv_heads = key_matrix.shape[1] // head // 8
        hidden = w_gate.shape[1]
        rows = w_q.shape[0]
        q_cols = heads * head
        k_cols = kv_heads * head
        part = hidden // 3 if hidden % 3072 == 0 else hidden
        chunks = [(start, part // 8) for start in range(0, hidden, part)]

        q_n, k_n, o_n = (w.shape[1] // 8 for w in (w_q, key_matrix, w_o))
        (attn_slot,) = pick_columns(
            [[(w_q, 0, q_n), (key_matrix, 0, k_n), (value_matrix, 0, k_n), (w_o, 0, o_n)]]
        )
        mlp_slots = pick_columns([[(w, start, n) for w in (w_gate, w_up, w_down)] for start, n in chunks])
        inputs = block_input.astype(F32)
        recip_attn = lax.rsqrt(jnp.mean(inputs * inputs, -1, keepdims=True) + EPSILON)
        normed_own = (inputs * recip_attn * attn_gain).astype(BF16)
        traded = [trade(slot) for slot in (attn_slot, *mlp_slots)]
        attn_weights, *mlp_weights = [gather_rows(v) for v in traded]
        qkv, w_o_cols = attn_weights[:, : q_n + 2 * k_n], attn_weights[:, q_n + 2 * k_n :]

        normed_rows = plane_gather(normed_own)
        grad_top = plane_gather(out_grad)
        notes = plane_notes(jnp.concatenate([segments, positions], 1))
        length = segments.shape[1]
        own_tokens = inputs.shape[0]
        tokens = normed_rows.shape[0]
        across = notes[:, None, :length]
        cosine, sine = rope_tables(notes[:, length:], head // 2)
        attention = (cosine, sine, across.reshape(tokens, 1), across, q_gain[None], k_gain[None])

        proj = dot(normed_rows, qkv)
        attended_rows = attention_forward(proj, *attention, heads, kv_heads)
        attended_rows, grad_top = lax.optimization_barrier((attended_rows, grad_top))
        mid = inputs + plane_scatter(lambda i, j: contract_cols(attended_rows[i:j], w_o_cols), own_tokens)
        recip_mlp = lax.rsqrt(jnp.mean(mid * mid, -1, keepdims=True) + EPSILON)
        mlp_in = plane_gather((mid * recip_mlp * mlp_gain).astype(BF16))

        acts, downs, owns, boths = [], [], [], []
        before = None
        for number, three in enumerate(mlp_weights):
            block = chunks[number][1]
            if number == 2:
                grad_top, owns[0] = after(grad_top, owns[0])
            weight = three[:, : 2 * block]
            pre = dot(mlp_in, weight)
            gate_pre, up_pre = pre[:, :block], pre[:, block:]
            sigma = jax.nn.sigmoid(gate_pre)
            silu_gate = gate_pre * sigma
            act = (silu_gate * up_pre).astype(BF16)
            grad_act = dot(grad_top, three[:, 2 * block :])
            grad_gate = (grad_act * up_pre * sigma * (1.0 + gate_pre * (1.0 - sigma))).astype(BF16)
            grad_up = (grad_act * silu_gate).astype(BF16)
            both = jnp.concatenate([grad_gate, grad_up], 1)
            own = jnp.concatenate([contract_rows(mlp_in, both), contract_rows(grad_top, act)], 1).astype(BF16)
            owns.append(own)
            boths.append(both)
            acts.append(act)
            downs.append(three[:, 2 * block :])
            if number < len(mlp_weights) - 1:
                part = contract_cols(both, weight)
                before = part if before is None else before + part
        grad_mlp_in = plane_scatter(
            lambda i, j: contract_cols(both[i:j], weight) + (0.0 if before is None else before[i:j]), own_tokens
        )
        grad_mid_part, mlp_gain_part = norm_back(grad_mlp_in, mid, recip_mlp, mlp_gain, 0)
        grad_mid = out_grad.astype(F32) + grad_mid_part
        mlp_rows = [queue_scatter(own) for own in owns[:-1]]
        grad_mid_b, owns[-1] = after(grad_mid.astype(BF16), owns[-1])
        grad_mid_b = plane_gather(grad_mid_b)
        act = jnp.concatenate(acts, 1)
        act, grad_mid_b = lax.optimization_barrier((act, grad_mid_b))
        down = jnp.concatenate(downs, 1)
        mlp_out = plane_scatter(lambda i, j: contract_cols(act[i:j], down), own_tokens)
        output = (mid + mlp_out).astype(BF16)
        attended_gradient = dot(grad_mid_b, w_o_cols).astype(BF16)
        own_o = contract_rows(grad_mid_b, attended_rows).astype(BF16)
        last_own = jnp.concatenate([owns[-1], own_o], 1)
        mlp_rows.append(queue_scatter(last_own))
        grad_qkv, head_gains = attention_backward(
            proj, *attention, attended_rows, attended_gradient, heads, kv_heads
        )
        own_qkv = contract_rows(normed_rows, grad_qkv).astype(BF16)
        mlp_grads = [hand_out(v) for v in mlp_rows[:-1]] + [None]
        grad_normed = plane_scatter(lambda i, j: contract_cols(grad_qkv[i:j], qkv), own_tokens)
        grad_in_part, attn_gain_part = norm_back(grad_normed, inputs, recip_attn, attn_gain, 0)
        grad_input = grad_mid + grad_in_part
        width = inputs.shape[1]
        sums = sum_everywhere(
            jnp.concatenate([attn_gain_part, mlp_gain_part, head_gains[0], head_gains[1]]).reshape(1, -1), far
        )[0]
        own_qkv, sums, grad_input, mlp_grads[:-1], mlp_rows[-1] = after(
            own_qkv, sums, grad_input, mlp_grads[:-1], mlp_rows[-1]
        )
        qkv_rows = queue_scatter(own_qkv)
        mlp_grads[-1] = hand_out(mlp_rows[-1])
        qkv_pair = hand_out(qkv_rows)
        last = len(chunks) - 1
        gate_pieces, up_pieces, down_pieces = ([(j, m * n, n) for j, (_, n) in enumerate(chunks)] for m in range(3))
        grad_w_gate, grad_w_up, grad_w_down, grad_w_o = spread(
            mlp_grads, [gate_pieces, up_pieces, down_pieces, [(last, 3 * chunks[last][1], o_n)]]
        )
        grad_w_q, grad_w_k, grad_w_v = spread([qkv_pair], [[(0, 0, q_n)], [(0, q_n, k_n)], [(0, q_n + k_n, k_n)]])
        return (
            output,
            grad_input,
            grad_w_q,
            grad_w_k,
            grad_w_v,
            grad_w_o,
            grad_w_gate,
            grad_w_up,
            grad_w_down,
            sums[:width],
            sums[width : 2 * width],
            sums[2 * width : 2 * width + head],
            sums[2 * width + head :],
        )

    return on_device


def solution(mesh):
    far = mesh.shape["shard"] // 4
    split = Mesh(mesh.devices.reshape(mesh.shape["rep"], far, 2, 2), ("rep", "far", "mid", "near"))
    tokens = P(("rep", "far", "mid", "near"), None)
    weights = P(("far", "mid", "near"), None)
    return jax.shard_map(
        build(far),
        mesh=split,
        in_specs=(tokens,) * 4 + (P(),) * 4 + (weights,) * 7,
        out_specs=(tokens,) * 2 + (weights,) * 7 + (P(),) * 4,
        check_vma=False,
    )
```

```python
import math

import jax
import jax.numpy as jnp
from jax import lax
from jax.experimental import pallas as pl
from jax.experimental.pallas import tpu as pltpu
from jax.sharding import Mesh
from jax.sharding import PartitionSpec as P

EPSILON = 1e-06
ROPE_BASE = 1000000.0
NEG_FILL = -1e30
F32 = jnp.float32
BF16 = jnp.bfloat16
SWAP = [(0, 1), (1, 0)]


def over_rep(v):
    return lax.ppermute(v, "rep", SWAP)


def over_mid(v):
    return lax.ppermute(v, "mid", SWAP)


def over_near(v):
    return lax.ppermute(v, "near", SWAP)


def plane_gather(own):
    half = own.shape[0] // 2
    from_rep = over_rep(own)
    from_mid = over_mid(own)
    top = over_mid(from_rep[:half])
    bottom = over_rep(from_mid[half:])
    mine = jnp.concatenate([own, from_rep, from_mid, top, bottom], 0)
    return jnp.concatenate([mine, over_near(mine)], 0)


def plane_scatter(partial, rows):
    half = rows // 2
    near = over_near(partial(4 * rows, 8 * rows).astype(BF16))
    part = partial(0, 4 * rows) + near.astype(F32)
    own, rep, mid, both = (part[i * rows : (i + 1) * rows] for i in range(4))
    first_rep = over_rep(jnp.concatenate([both[:half], rep[:half]], 0).astype(BF16))
    first_mid = over_mid(jnp.concatenate([both[half:], mid[half:]], 0).astype(BF16))
    last_mid = over_mid((mid[:half] + first_rep[:half].astype(F32)).astype(BF16))
    last_rep = over_rep((rep[half:] + first_mid[:half].astype(F32)).astype(BF16))
    top = own[:half] + first_rep[half:].astype(F32) + last_mid.astype(F32)
    bottom = own[half:] + last_rep.astype(F32) + first_mid[half:].astype(F32)
    return jnp.concatenate([top, bottom], 0)


def pick_columns(groups):
    side = lax.axis_index("rep").astype(jnp.int32).reshape(1)
    members = [m for group in groups for m in group]
    rows = members[0][0].shape[0]
    widths = [sum(n for _, _, n in group) for group in groups]

    def kernel(side_ref, *refs):
        sources = iter(refs[: len(members)])
        for group, out in zip(groups, refs[len(members) :]):
            at = 0
            for _, _, n in group:
                source = next(sources)
                for block in range(4):
                    out[block, :, at : at + n] = source[:, block * n : (block + 1) * n]
                at += n

    def half(start, n):
        return pl.BlockSpec((rows, 4 * n), lambda i, side_ref: (0, start // (4 * n) + side_ref[0]))

    return pl.pallas_call(
        kernel,
        grid_spec=pltpu.PrefetchScalarGridSpec(
            num_scalar_prefetch=1,
            grid=(1,),
            in_specs=[half(start, n) for _, start, n in members],
            out_specs=[pl.BlockSpec((4, rows, w), lambda i, side_ref: (0, 0, 0)) for w in widths],
        ),
        out_shape=[jax.ShapeDtypeStruct((4, rows, w), BF16) for w in widths],
        compiler_params=pltpu.CompilerParams(vmem_limit_bytes=20 << 20),
        name="pick_columns",
    )(side, *[m for m, _, _ in members])


def trade(blocks):
    return lax.all_to_all(blocks, ("mid", "near"), 0, 0)


def gather_rows(blocks):
    four, rows, n = blocks.shape
    return lax.all_gather(blocks.reshape(four * rows, n), "far", axis=0, tiled=True)


def queue_scatter(parts):
    return lax.psum_scatter(parts, "far", scatter_dimension=0, tiled=True)


def hand_out(mine):
    mine = trade(mine.reshape(4, mine.shape[0] // 4, -1))
    return (mine, over_rep(mine))


def spread(pairs, outs):
    side = lax.axis_index("rep").astype(jnp.int32).reshape(1)
    rows = pairs[0][0].shape[1]
    columns = [sum(8 * n for _, _, n in pieces) for pieces in outs]

    def kernel(side_ref, *refs):
        first = side_ref[0] == 0
        for out, pieces in zip(refs[2 * len(pairs) :], outs):
            at = 0
            for pair, start, n in pieces:
                own, other = refs[2 * pair], refs[2 * pair + 1]
                for block in range(4):
                    a = own[block, :, start : start + n].astype(F32)
                    b = other[block, :, start : start + n].astype(F32)
                    out[:, at + block * n : at + (block + 1) * n] = jnp.where(first, a, b)
                    out[:, at + (4 + block) * n : at + (5 + block) * n] = jnp.where(first, b, a)
                at += 8 * n

    return pl.pallas_call(
        kernel,
        in_specs=[pl.BlockSpec(memory_space=pltpu.SMEM)] + [pl.BlockSpec(memory_space=pltpu.VMEM)] * (2 * len(pairs)),
        out_specs=[pl.BlockSpec(memory_space=pltpu.VMEM)] * len(outs),
        out_shape=[jax.ShapeDtypeStruct((rows, c), F32) for c in columns],
        compiler_params=pltpu.CompilerParams(vmem_limit_bytes=40 << 20),
        name="spread",
    )(side, *[v for pair in pairs for v in pair])


def sum_everywhere(v, size):
    for axis in ("near", "mid", "rep"):
        v = v + lax.ppermute(v, axis, SWAP)
    if size & (size - 1):
        return lax.psum(v, "far")
    step = 1
    while step < size:
        v = v + lax.ppermute(v, "far", [(i, i ^ step) for i in range(size)])
        step *= 2
    return v


def after(*values):
    return lax.optimization_barrier(values)


def rope_tables(positions, half):
    freq = jnp.exp(jnp.arange(half, dtype=F32) * (-math.log(ROPE_BASE) / half))
    angles = positions.reshape(-1).astype(F32)[:, None] * freq
    cosine, sine = (jnp.cos(angles), jnp.sin(angles))
    return (jnp.concatenate([cosine, cosine], 1), jnp.concatenate([-sine, sine], 1))


def norm_back(grads, inputs, recip, gain, axes):
    normal = inputs * recip
    scaled = grads * gain
    gain_grad = jnp.sum(grads * normal, axis=axes)
    input_grad = recip * (scaled - normal * jnp.mean(scaled * normal, -1, keepdims=True))
    return (input_grad, gain_grad)


def dot(left, right):
    return jnp.dot(left, right, preferred_element_type=F32)


def contract_rows(left, right):
    return lax.dot_general(left, right, (((0,), (0,)), ((), ())), preferred_element_type=F32)


def contract_cols(left, right):
    return lax.dot_general(left, right, (((1,), (1,)), ((), ())), preferred_element_type=F32)


def swap_halves(v):
    half = v.shape[-1] // 2
    return jnp.concatenate([v[:, half:], v[:, :half]], -1)


def unit(u):
    recip = lax.rsqrt(jnp.mean(u * u, -1, keepdims=True) + EPSILON)
    return (u * recip, recip)


def sequence_state(proj_ref, cosine_ref, sine_ref, down_ref, across_ref, head):
    length = proj_ref.shape[0]
    later = lax.broadcasted_iota(jnp.int32, (length, length), 0)
    earlier = lax.broadcasted_iota(jnp.int32, (length, length), 1)
    mask = (down_ref[...] == across_ref[0]) & (earlier <= later)
    cosine, sine = cosine_ref[...], sine_ref[...]

    def turned(v):
        return v * cosine + swap_halves(v) * sine

    def turned_back(v):
        return v * cosine - swap_halves(v) * sine

    def columns(i):
        return proj_ref[:, i * head : (i + 1) * head]

    return (mask, turned, turned_back, columns)


def masked_scores(query, key, mask, head):
    return jnp.where(mask, contract_cols(query, key) * head ** (-0.5), NEG_FILL)


def attention_forward(proj, cosine, sine, down, across, q_gain, k_gain, heads, kv_heads):
    head = q_gain.shape[1]
    sequences, _, length = across.shape
    groups = heads // kv_heads

    def kernel(proj_ref, cosine_ref, sine_ref, down_ref, across_ref, q_gain_ref, k_gain_ref, out_ref):
        mask, turned, _, columns = sequence_state(proj_ref, cosine_ref, sine_ref, down_ref, across_ref, head)
        for kv in range(kv_heads):
            key = turned(unit(columns(heads + kv))[0] * k_gain_ref[...]).astype(BF16)
            value = columns(heads + kv_heads + kv).astype(BF16)
            for h in range(kv * groups, (kv + 1) * groups):
                query = turned(unit(columns(h))[0] * q_gain_ref[...]).astype(BF16)
                scores = masked_scores(query, key, mask, head)
                expo = jnp.exp(scores - jnp.max(scores, -1, keepdims=True))
                probs = (expo / jnp.sum(expo, -1, keepdims=True)).astype(BF16)
                out_ref[:, h * head : (h + 1) * head] = dot(probs, value).astype(BF16)

    row = lambda n: pl.BlockSpec((length, n), lambda i: (i, 0))
    fixed = pl.BlockSpec((1, head), lambda i: (0, 0))
    return pl.pallas_call(
        kernel,
        grid=(sequences,),
        in_specs=[row(proj.shape[1]), row(head), row(head), row(1)]
        + [pl.BlockSpec((1, 1, length), lambda i: (i, 0, 0)), fixed, fixed],
        out_specs=row(heads * head),
        out_shape=jax.ShapeDtypeStruct((proj.shape[0], heads * head), BF16),
        compiler_params=pltpu.CompilerParams(vmem_limit_bytes=6 << 20),
        name="attention_forward",
    )(proj, cosine, sine, down, across, q_gain, k_gain)


def attention_backward(proj, cosine, sine, down, across, q_gain, k_gain, attended, attended_grad, heads, kv_heads):
    head = q_gain.shape[1]
    sequences, _, length = across.shape
    groups = heads // kv_heads
    scale = head ** (-0.5)

    def kernel(
        proj_ref,
        cosine_ref,
        sine_ref,
        down_ref,
        across_ref,
        q_gain_ref,
        k_gain_ref,
        attended_ref,
        grad_ref,
        out_ref,
        gains_ref,
    ):
        mask, turned, turned_back, columns = sequence_state(
            proj_ref, cosine_ref, sine_ref, down_ref, across_ref, head
        )

        @pl.when(pl.program_id(0) == 0)
        def _():
            gains_ref[...] = jnp.zeros_like(gains_ref)

        def put(i, v):
            out_ref[:, i * head : (i + 1) * head] = v.astype(BF16)

        def norm_grad(i, grads, normal, recip, gain, row):
            scaled = grads * gain
            gains_ref[row : row + 1, :] += jnp.sum(grads * normal, 0, keepdims=True)
            put(i, recip * (scaled - normal * jnp.mean(scaled * normal, -1, keepdims=True)))

        for kv in range(kv_heads):
            key_unit, key_recip = unit(columns(heads + kv))
            key = turned(key_unit * k_gain_ref[...]).astype(BF16)
            value = columns(heads + kv_heads + kv).astype(BF16)
            grad_value = jnp.zeros((length, head), F32)
            grad_key = jnp.zeros((length, head), F32)
            for h in range(kv * groups, (kv + 1) * groups):
                query_unit, query_recip = unit(columns(h))
                query = turned(query_unit * q_gain_ref[...]).astype(BF16)
                scores = masked_scores(query, key, mask, head)
                top = jnp.max(scores, -1, keepdims=True)
                log_total = top + jnp.log(jnp.sum(jnp.exp(scores - top), -1, keepdims=True))
                probs = jnp.where(mask, jnp.exp(scores - log_total), 0.0)
                grad = grad_ref[:, h * head : (h + 1) * head]
                grad_value += contract_rows(probs.astype(BF16), grad)
                complete = attended_ref[:, h * head : (h + 1) * head].astype(F32)
                delta = jnp.sum(grad.astype(F32) * complete, -1, keepdims=True)
                grad_scores = (probs * (contract_cols(grad, value) - delta)).astype(BF16)
                grad_query = dot(grad_scores, key) * scale
                grad_key += contract_rows(grad_scores, query)
                norm_grad(h, turned_back(grad_query), query_unit, query_recip, q_gain_ref[...], 0)
            norm_grad(heads + kv, turned_back(grad_key * scale), key_unit, key_recip, k_gain_ref[...], 1)
            put(heads + kv_heads + kv, grad_value)

    row = lambda n: pl.BlockSpec((length, n), lambda i: (i, 0))
    fixed = pl.BlockSpec((1, head), lambda i: (0, 0))
    return pl.pallas_call(
        kernel,
        grid=(sequences,),
        in_specs=[row(proj.shape[1]), row(head), row(head), row(1)]
        + [pl.BlockSpec((1, 1, length), lambda i: (i, 0, 0)), fixed, fixed]
        + [row(heads * head), row(heads * head)],
        out_specs=[row(proj.shape[1]), pl.BlockSpec((8, head), lambda i: (0, 0))],
        out_shape=[jax.ShapeDtypeStruct(proj.shape, BF16), jax.ShapeDtypeStruct((8, head), F32)],
        compiler_params=pltpu.CompilerParams(vmem_limit_bytes=8 << 20),
        name="attention_backward",
    )(proj, cosine, sine, down, across, q_gain, k_gain, attended, attended_grad)


def plane_notes(own):
    pair = jnp.concatenate([own, over_near(own)], 0)
    four = jnp.concatenate([pair, over_mid(pair)], 0)
    eight = jnp.concatenate([four, over_rep(four)], 0)
    return jnp.concatenate([eight[i : i + 1] for i in (0, 4, 2, 6, 1, 5, 3, 7)], 0)


def build(far):
    def on_device(
        block_input,
        out_grad,
        segments,
        positions,
        attn_gain,
        mlp_gain,
        q_gain,
        k_gain,
        w_q,
        key_matrix,
        value_matrix,
        w_o,
        w_gate,
        w_up,
        w_down,
    ):
        head = q_gain.shape[0]
        heads = w_q.shape[1] // head // 8
        kv_heads = key_matrix.shape[1] // head // 8
        hidden = w_gate.shape[1]
        rows = w_q.shape[0]
        q_cols = heads * head
        k_cols = kv_heads * head
        part = hidden // 3 if hidden % 3072 == 0 else hidden
        chunks = [(start, part // 8) for start in range(0, hidden, part)]

        q_n, k_n, o_n = (w.shape[1] // 8 for w in (w_q, key_matrix, w_o))
        (attn_slot,) = pick_columns(
            [[(w_q, 0, q_n), (key_matrix, 0, k_n), (value_matrix, 0, k_n), (w_o, 0, o_n)]]
        )
        mlp_slots = pick_columns(
            [[(w, start, n) for start, n in part for w in (w_gate, w_up, w_down)] for part in (chunks[:-1], chunks[-1:]) if part]
        )
        inputs = block_input.astype(F32)
        recip_attn = lax.rsqrt(jnp.mean(inputs * inputs, -1, keepdims=True) + EPSILON)
        normed_own = (inputs * recip_attn * attn_gain).astype(BF16)
        traded = [trade(slot) for slot in (attn_slot, *mlp_slots)]
        attn_weights, *gathered = [gather_rows(v) for v in traded]
        mlp_weights = []
        for part in gathered:
            step = 3 * chunks[0][1]
            mlp_weights += [part[:, at : at + step] for at in range(0, part.shape[1], step)]
        qkv, w_o_cols = attn_weights[:, : q_n + 2 * k_n], attn_weights[:, q_n + 2 * k_n :]

        normed_rows = plane_gather(normed_own)
        grad_top = plane_gather(out_grad)
        notes = plane_notes(jnp.concatenate([segments, positions], 1))
        length = segments.shape[1]
        own_tokens = inputs.shape[0]
        tokens = normed_rows.shape[0]
        across = notes[:, None, :length]
        cosine, sine = rope_tables(notes[:, length:], head // 2)
        attention = (cosine, sine, across.reshape(tokens, 1), across, q_gain[None], k_gain[None])

        proj = dot(normed_rows, qkv)
        attended_rows = attention_forward(proj, *attention, heads, kv_heads)
        attended_rows, grad_top = lax.optimization_barrier((attended_rows, grad_top))
        mid = inputs + plane_scatter(lambda i, j: contract_cols(attended_rows[i:j], w_o_cols), own_tokens)
        recip_mlp = lax.rsqrt(jnp.mean(mid * mid, -1, keepdims=True) + EPSILON)
        mlp_in = plane_gather((mid * recip_mlp * mlp_gain).astype(BF16))

        acts, downs, owns, boths = [], [], [], []
        before = None
        for number, three in enumerate(mlp_weights):
            block = chunks[number][1]
            if number == 2:
                three, owns[0] = after(three, owns[0])
            weight = three[:, : 2 * block]
            pre = dot(mlp_in, weight)
            gate_pre, up_pre = pre[:, :block], pre[:, block:]
            sigma = jax.nn.sigmoid(gate_pre)
            silu_gate = gate_pre * sigma
            act = (silu_gate * up_pre).astype(BF16)
            grad_act = dot(grad_top, three[:, 2 * block :])
            grad_gate = (grad_act * up_pre * sigma * (1.0 + gate_pre * (1.0 - sigma))).astype(BF16)
            grad_up = (grad_act * silu_gate).astype(BF16)
            both = jnp.concatenate([grad_gate, grad_up], 1)
            own = jnp.concatenate([contract_rows(mlp_in, both), contract_rows(grad_top, act)], 1).astype(BF16)
            owns.append(own)
            boths.append(both)
            acts.append(act)
            downs.append(three[:, 2 * block :])
            if number < len(mlp_weights) - 1:
                part = contract_cols(both, weight)
                before = part if before is None else before + part
        grad_mlp_in = plane_scatter(
            lambda i, j: contract_cols(both[i:j], weight) + (0.0 if before is None else before[i:j]), own_tokens
        )
        grad_mid_part, mlp_gain_part = norm_back(grad_mlp_in, mid, recip_mlp, mlp_gain, 0)
        grad_mid = out_grad.astype(F32) + grad_mid_part
        mlp_rows = [queue_scatter(own) for own in owns[:-1]]
        grad_mid_b, owns[-1] = after(grad_mid.astype(BF16), owns[-1])
        grad_mid_b = plane_gather(grad_mid_b)
        act = jnp.concatenate(acts, 1)
        act, grad_mid_b = lax.optimization_barrier((act, grad_mid_b))
        down = jnp.concatenate(downs, 1)
        mlp_out = plane_scatter(lambda i, j: contract_cols(act[i:j], down), own_tokens)
        output = (mid + mlp_out).astype(BF16)
        attended_gradient = dot(grad_mid_b, w_o_cols).astype(BF16)
        own_o = contract_rows(grad_mid_b, attended_rows).astype(BF16)
        last_own = jnp.concatenate([owns[-1], own_o], 1)
        mlp_rows.append(queue_scatter(last_own))
        grad_qkv, head_gains = attention_backward(
            proj, *attention, attended_rows, attended_gradient, heads, kv_heads
        )
        own_qkv = contract_rows(normed_rows, grad_qkv).astype(BF16)
        mlp_grads = [hand_out(v) for v in mlp_rows[:-1]] + [None]
        grad_normed = plane_scatter(lambda i, j: contract_cols(grad_qkv[i:j], qkv), own_tokens)
        grad_in_part, attn_gain_part = norm_back(grad_normed, inputs, recip_attn, attn_gain, 0)
        grad_input = grad_mid + grad_in_part
        width = inputs.shape[1]
        sums = sum_everywhere(
            jnp.concatenate([attn_gain_part, mlp_gain_part, head_gains[0], head_gains[1]]).reshape(1, -1), far
        )[0]
        own_qkv, sums, grad_input, mlp_grads[:-1], mlp_rows[-1] = after(
            own_qkv, sums, grad_input, mlp_grads[:-1], mlp_rows[-1]
        )
        qkv_rows = queue_scatter(own_qkv)
        mlp_grads[-1] = hand_out(mlp_rows[-1])
        qkv_pair = hand_out(qkv_rows)
        last = len(chunks) - 1
        gate_pieces, up_pieces, down_pieces = ([(j, m * n, n) for j, (_, n) in enumerate(chunks)] for m in range(3))
        grad_w_gate, grad_w_up, grad_w_down, grad_w_o = spread(
            mlp_grads, [gate_pieces, up_pieces, down_pieces, [(last, 3 * chunks[last][1], o_n)]]
        )
        grad_w_q, grad_w_k, grad_w_v = spread([qkv_pair], [[(0, 0, q_n)], [(0, q_n, k_n)], [(0, q_n + k_n, k_n)]])
        return (
            output,
            grad_input,
            grad_w_q,
            grad_w_k,
            grad_w_v,
            grad_w_o,
            grad_w_gate,
            grad_w_up,
            grad_w_down,
            sums[:width],
            sums[width : 2 * width],
            sums[2 * width : 2 * width + head],
            sums[2 * width + head :],
        )

    return on_device


def solution(mesh):
    far = mesh.shape["shard"] // 4
    split = Mesh(mesh.devices.reshape(mesh.shape["rep"], far, 2, 2), ("rep", "far", "mid", "near"))
    tokens = P(("rep", "far", "mid", "near"), None)
    weights = P(("far", "mid", "near"), None)
    return jax.shard_map(
        build(far),
        mesh=split,
        in_specs=(tokens,) * 4 + (P(),) * 4 + (weights,) * 7,
        out_specs=(tokens,) * 2 + (weights,) * 7 + (P(),) * 4,
        check_vma=False,
    )
```

```python
import math

import jax
import jax.numpy as jnp
from jax import lax
from jax.experimental import pallas as pl
from jax.experimental.pallas import tpu as pltpu
from jax.sharding import Mesh
from jax.sharding import PartitionSpec as P

EPSILON = 1e-06
ROPE_BASE = 1000000.0
NEG_FILL = -1e30
F32 = jnp.float32
BF16 = jnp.bfloat16
SWAP = [(0, 1), (1, 0)]


def over_rep(v):
    return lax.ppermute(v, "rep", SWAP)


def over_mid(v):
    return lax.ppermute(v, "mid", SWAP)


def over_near(v):
    return lax.ppermute(v, "near", SWAP)


def plane_gather(own):
    half = own.shape[0] // 2
    from_rep = over_rep(own)
    from_mid = over_mid(own)
    top = over_mid(from_rep[:half])
    bottom = over_rep(from_mid[half:])
    mine = jnp.concatenate([own, from_rep, from_mid, top, bottom], 0)
    return jnp.concatenate([mine, over_near(mine)], 0)


def plane_scatter(partial, rows):
    half = rows // 2
    near = over_near(partial(4 * rows, 8 * rows).astype(BF16))
    part = partial(0, 4 * rows) + near.astype(F32)
    own, rep, mid, both = (part[i * rows : (i + 1) * rows] for i in range(4))
    first_rep = over_rep(jnp.concatenate([both[:half], rep[:half]], 0).astype(BF16))
    first_mid = over_mid(jnp.concatenate([both[half:], mid[half:]], 0).astype(BF16))
    last_mid = over_mid((mid[:half] + first_rep[:half].astype(F32)).astype(BF16))
    last_rep = over_rep((rep[half:] + first_mid[:half].astype(F32)).astype(BF16))
    top = own[:half] + first_rep[half:].astype(F32) + last_mid.astype(F32)
    bottom = own[half:] + last_rep.astype(F32) + first_mid[half:].astype(F32)
    return jnp.concatenate([top, bottom], 0)


def pick_columns(groups):
    side = lax.axis_index("rep").astype(jnp.int32).reshape(1)
    members = [m for group in groups for m in group]
    rows = members[0][0].shape[0]
    widths = [sum(n for _, _, n in group) for group in groups]

    tile = math.gcd(rows, 16)

    def kernel(side_ref, *refs):
        def some(step, carry):
            span = pl.ds(pl.multiple_of(step * tile, tile), tile)
            sources = iter(refs[: len(members)])
            for group, out in zip(groups, refs[len(members) :]):
                at = 0
                for _, _, n in group:
                    source = next(sources)
                    for block in range(4):
                        out[block, span, at : at + n] = source[span, block * n : (block + 1) * n]
                    at += n
            return carry

        lax.fori_loop(0, rows // tile, some, 0)

    def half(start, n):
        return pl.BlockSpec((rows, 4 * n), lambda i, side_ref: (0, start // (4 * n) + side_ref[0]))

    return pl.pallas_call(
        kernel,
        grid_spec=pltpu.PrefetchScalarGridSpec(
            num_scalar_prefetch=1,
            grid=(1,),
            in_specs=[half(start, n) for _, start, n in members],
            out_specs=[pl.BlockSpec((4, rows, w), lambda i, side_ref: (0, 0, 0)) for w in widths],
        ),
        out_shape=[jax.ShapeDtypeStruct((4, rows, w), BF16) for w in widths],
        compiler_params=pltpu.CompilerParams(vmem_limit_bytes=20 << 20),
        name="pick_columns",
    )(side, *[m for m, _, _ in members])


def trade(blocks):
    return lax.all_to_all(blocks, ("mid", "near"), 0, 0)


def gather_rows(blocks):
    four, rows, n = blocks.shape
    return lax.all_gather(blocks.reshape(four * rows, n), "far", axis=0, tiled=True)


def queue_scatter(parts):
    return lax.psum_scatter(parts, "far", scatter_dimension=0, tiled=True)


def hand_out(mine):
    return trade(mine.reshape(4, mine.shape[0] // 4, -1))


def both_sides(mine):
    return (mine, over_rep(mine))


def spread(pairs, outs):
    side = lax.axis_index("rep").astype(jnp.int32).reshape(1)
    rows = pairs[0][0].shape[1]
    columns = [sum(8 * n for _, _, n in pieces) for pieces in outs]

    tile = math.gcd(rows, 16)

    def kernel(side_ref, *refs):
        first = side_ref[0] == 0

        def some(step, carry):
            span = pl.ds(pl.multiple_of(step * tile, tile), tile)
            for out, pieces in zip(refs[2 * len(pairs) :], outs):
                at = 0
                for pair, start, n in pieces:
                    own, other = refs[2 * pair], refs[2 * pair + 1]
                    for block in range(4):
                        a = own[block, span, start : start + n].astype(F32)
                        b = other[block, span, start : start + n].astype(F32)
                        out[span, at + block * n : at + (block + 1) * n] = jnp.where(first, a, b)
                        out[span, at + (4 + block) * n : at + (5 + block) * n] = jnp.where(first, b, a)
                    at += 8 * n
            return carry

        lax.fori_loop(0, rows // tile, some, 0)

    return pl.pallas_call(
        kernel,
        in_specs=[pl.BlockSpec(memory_space=pltpu.SMEM)] + [pl.BlockSpec(memory_space=pltpu.VMEM)] * (2 * len(pairs)),
        out_specs=[pl.BlockSpec(memory_space=pltpu.VMEM)] * len(outs),
        out_shape=[jax.ShapeDtypeStruct((rows, c), F32) for c in columns],
        compiler_params=pltpu.CompilerParams(vmem_limit_bytes=40 << 20),
        name="spread",
    )(side, *[v for pair in pairs for v in pair])


def sum_everywhere(v, size):
    for axis in ("near", "mid", "rep"):
        v = v + lax.ppermute(v, axis, SWAP)
    if size & (size - 1):
        return lax.psum(v, "far")
    step = 1
    while step < size:
        v = v + lax.ppermute(v, "far", [(i, i ^ step) for i in range(size)])
        step *= 2
    return v


def after(*values):
    return lax.optimization_barrier(values)


def rope_tables(positions, half):
    freq = jnp.exp(jnp.arange(half, dtype=F32) * (-math.log(ROPE_BASE) / half))
    angles = positions.reshape(-1).astype(F32)[:, None] * freq
    cosine, sine = (jnp.cos(angles), jnp.sin(angles))
    return (jnp.concatenate([cosine, cosine], 1), jnp.concatenate([-sine, sine], 1))


def norm_back(grads, inputs, recip, gain, axes):
    normal = inputs * recip
    scaled = grads * gain
    gain_grad = jnp.sum(grads * normal, axis=axes)
    input_grad = recip * (scaled - normal * jnp.mean(scaled * normal, -1, keepdims=True))
    return (input_grad, gain_grad)


def dot(left, right):
    return jnp.dot(left, right, preferred_element_type=F32)


def contract_rows(left, right):
    return lax.dot_general(left, right, (((0,), (0,)), ((), ())), preferred_element_type=F32)


def contract_cols(left, right):
    return lax.dot_general(left, right, (((1,), (1,)), ((), ())), preferred_element_type=F32)


def swap_halves(v):
    half = v.shape[-1] // 2
    return jnp.concatenate([v[:, half:], v[:, :half]], -1)


def unit(u):
    recip = lax.rsqrt(jnp.mean(u * u, -1, keepdims=True) + EPSILON)
    return (u * recip, recip)


def sequence_state(proj_ref, cosine_ref, sine_ref, down_ref, across_ref, head):
    length = proj_ref.shape[0]
    later = lax.broadcasted_iota(jnp.int32, (length, length), 0)
    earlier = lax.broadcasted_iota(jnp.int32, (length, length), 1)
    mask = (down_ref[...] == across_ref[0]) & (earlier <= later)
    cosine, sine = cosine_ref[...], sine_ref[...]

    def turned(v):
        return v * cosine + swap_halves(v) * sine

    def turned_back(v):
        return v * cosine - swap_halves(v) * sine

    def columns(i):
        return proj_ref[:, i * head : (i + 1) * head]

    return (mask, turned, turned_back, columns)


def masked_scores(query, key, mask, head):
    return jnp.where(mask, contract_cols(query, key) * head ** (-0.5), NEG_FILL)


def attention_forward(proj, cosine, sine, down, across, q_gain, k_gain, heads, kv_heads):
    head = q_gain.shape[1]
    sequences, _, length = across.shape
    groups = heads // kv_heads

    def kernel(proj_ref, cosine_ref, sine_ref, down_ref, across_ref, q_gain_ref, k_gain_ref, out_ref):
        mask, turned, _, columns = sequence_state(proj_ref, cosine_ref, sine_ref, down_ref, across_ref, head)
        for kv in range(kv_heads):
            key = turned(unit(columns(heads + kv))[0] * k_gain_ref[...]).astype(BF16)
            value = columns(heads + kv_heads + kv).astype(BF16)
            for h in range(kv * groups, (kv + 1) * groups):
                query = turned(unit(columns(h))[0] * q_gain_ref[...]).astype(BF16)
                scores = masked_scores(query, key, mask, head)
                expo = jnp.exp(scores - jnp.max(scores, -1, keepdims=True))
                probs = (expo / jnp.sum(expo, -1, keepdims=True)).astype(BF16)
                out_ref[:, h * head : (h + 1) * head] = dot(probs, value).astype(BF16)

    row = lambda n: pl.BlockSpec((length, n), lambda i: (i, 0))
    fixed = pl.BlockSpec((1, head), lambda i: (0, 0))
    return pl.pallas_call(
        kernel,
        grid=(sequences,),
        in_specs=[row(proj.shape[1]), row(head), row(head), row(1)]
        + [pl.BlockSpec((1, 1, length), lambda i: (i, 0, 0)), fixed, fixed],
        out_specs=row(heads * head),
        out_shape=jax.ShapeDtypeStruct((proj.shape[0], heads * head), BF16),
        compiler_params=pltpu.CompilerParams(vmem_limit_bytes=6 << 20),
        name="attention_forward",
    )(proj, cosine, sine, down, across, q_gain, k_gain)


def attention_backward(proj, cosine, sine, down, across, q_gain, k_gain, attended, attended_grad, heads, kv_heads):
    head = q_gain.shape[1]
    sequences, _, length = across.shape
    groups = heads // kv_heads
    scale = head ** (-0.5)

    def kernel(
        proj_ref,
        cosine_ref,
        sine_ref,
        down_ref,
        across_ref,
        q_gain_ref,
        k_gain_ref,
        attended_ref,
        grad_ref,
        out_ref,
        gains_ref,
    ):
        mask, turned, turned_back, columns = sequence_state(
            proj_ref, cosine_ref, sine_ref, down_ref, across_ref, head
        )

        @pl.when(pl.program_id(0) == 0)
        def _():
            gains_ref[...] = jnp.zeros_like(gains_ref)

        def put(i, v):
            out_ref[:, i * head : (i + 1) * head] = v.astype(BF16)

        def norm_grad(i, grads, normal, recip, gain, row):
            scaled = grads * gain
            gains_ref[row : row + 1, :] += jnp.sum(grads * normal, 0, keepdims=True)
            put(i, recip * (scaled - normal * jnp.mean(scaled * normal, -1, keepdims=True)))

        for kv in range(kv_heads):
            key_unit, key_recip = unit(columns(heads + kv))
            key = turned(key_unit * k_gain_ref[...]).astype(BF16)
            value = columns(heads + kv_heads + kv).astype(BF16)
            grad_value = jnp.zeros((length, head), F32)
            grad_key = jnp.zeros((length, head), F32)
            for h in range(kv * groups, (kv + 1) * groups):
                query_unit, query_recip = unit(columns(h))
                query = turned(query_unit * q_gain_ref[...]).astype(BF16)
                scores = masked_scores(query, key, mask, head)
                top = jnp.max(scores, -1, keepdims=True)
                log_total = top + jnp.log(jnp.sum(jnp.exp(scores - top), -1, keepdims=True))
                probs = jnp.where(mask, jnp.exp(scores - log_total), 0.0)
                grad = grad_ref[:, h * head : (h + 1) * head]
                grad_value += contract_rows(probs.astype(BF16), grad)
                complete = attended_ref[:, h * head : (h + 1) * head].astype(F32)
                delta = jnp.sum(grad.astype(F32) * complete, -1, keepdims=True)
                grad_scores = (probs * (contract_cols(grad, value) - delta)).astype(BF16)
                grad_query = dot(grad_scores, key) * scale
                grad_key += contract_rows(grad_scores, query)
                norm_grad(h, turned_back(grad_query), query_unit, query_recip, q_gain_ref[...], 0)
            norm_grad(heads + kv, turned_back(grad_key * scale), key_unit, key_recip, k_gain_ref[...], 1)
            put(heads + kv_heads + kv, grad_value)

    row = lambda n: pl.BlockSpec((length, n), lambda i: (i, 0))
    fixed = pl.BlockSpec((1, head), lambda i: (0, 0))
    return pl.pallas_call(
        kernel,
        grid=(sequences,),
        in_specs=[row(proj.shape[1]), row(head), row(head), row(1)]
        + [pl.BlockSpec((1, 1, length), lambda i: (i, 0, 0)), fixed, fixed]
        + [row(heads * head), row(heads * head)],
        out_specs=[row(proj.shape[1]), pl.BlockSpec((8, head), lambda i: (0, 0))],
        out_shape=[jax.ShapeDtypeStruct(proj.shape, BF16), jax.ShapeDtypeStruct((8, head), F32)],
        compiler_params=pltpu.CompilerParams(vmem_limit_bytes=8 << 20),
        name="attention_backward",
    )(proj, cosine, sine, down, across, q_gain, k_gain, attended, attended_grad)


def plane_notes(own):
    pair = jnp.concatenate([own, over_near(own)], 0)
    four = jnp.concatenate([pair, over_mid(pair)], 0)
    eight = jnp.concatenate([four, over_rep(four)], 0)
    return jnp.concatenate([eight[i : i + 1] for i in (0, 4, 2, 6, 1, 5, 3, 7)], 0)


def build(far):
    def on_device(
        block_input,
        out_grad,
        segments,
        positions,
        attn_gain,
        mlp_gain,
        q_gain,
        k_gain,
        w_q,
        key_matrix,
        value_matrix,
        w_o,
        w_gate,
        w_up,
        w_down,
    ):
        head = q_gain.shape[0]
        heads = w_q.shape[1] // head // 8
        kv_heads = key_matrix.shape[1] // head // 8
        hidden = w_gate.shape[1]
        rows = w_q.shape[0]
        q_cols = heads * head
        k_cols = kv_heads * head
        part = hidden // 3 if hidden % 3072 == 0 else hidden
        chunks = [(start, part // 8) for start in range(0, hidden, part)]

        q_n, k_n, o_n = (w.shape[1] // 8 for w in (w_q, key_matrix, w_o))
        (attn_slot,) = pick_columns(
            [[(w_q, 0, q_n), (key_matrix, 0, k_n), (value_matrix, 0, k_n), (w_o, 0, o_n)]]
        )
        mlp_slots = pick_columns(
            [[(w, start, n) for start, n in part for w in (w_gate, w_up, w_down)] for part in (chunks[:-1], chunks[-1:]) if part]
        )
        inputs = block_input.astype(F32)
        recip_attn = lax.rsqrt(jnp.mean(inputs * inputs, -1, keepdims=True) + EPSILON)
        normed_own = (inputs * recip_attn * attn_gain).astype(BF16)
        traded = [trade(slot) for slot in (attn_slot, *mlp_slots)]
        attn_weights, *gathered = [gather_rows(v) for v in traded]
        mlp_weights = []
        for part in gathered:
            step = 3 * chunks[0][1]
            mlp_weights += [part[:, at : at + step] for at in range(0, part.shape[1], step)]
        qkv, w_o_cols = attn_weights[:, : q_n + 2 * k_n], attn_weights[:, q_n + 2 * k_n :]

        normed_rows = plane_gather(normed_own)
        grad_top = plane_gather(out_grad)
        notes = plane_notes(jnp.concatenate([segments, positions], 1))
        length = segments.shape[1]
        own_tokens = inputs.shape[0]
        tokens = normed_rows.shape[0]
        across = notes[:, None, :length]
        cosine, sine = rope_tables(notes[:, length:], head // 2)
        attention = (cosine, sine, across.reshape(tokens, 1), across, q_gain[None], k_gain[None])

        proj = dot(normed_rows, qkv)
        attended_rows = attention_forward(proj, *attention, heads, kv_heads)
        attended_rows, grad_top = lax.optimization_barrier((attended_rows, grad_top))
        mid = inputs + plane_scatter(lambda i, j: contract_cols(attended_rows[i:j], w_o_cols), own_tokens)
        recip_mlp = lax.rsqrt(jnp.mean(mid * mid, -1, keepdims=True) + EPSILON)
        mlp_in = plane_gather((mid * recip_mlp * mlp_gain).astype(BF16))

        acts, downs, owns, boths = [], [], [], []
        before = None
        for number, three in enumerate(mlp_weights):
            block = chunks[number][1]
            if number == 2:
                three, owns[0] = after(three, owns[0])
            weight = three[:, : 2 * block]
            pre = dot(mlp_in, weight)
            gate_pre, up_pre = pre[:, :block], pre[:, block:]
            sigma = jax.nn.sigmoid(gate_pre)
            silu_gate = gate_pre * sigma
            act = (silu_gate * up_pre).astype(BF16)
            grad_act = dot(grad_top, three[:, 2 * block :])
            grad_gate = (grad_act * up_pre * sigma * (1.0 + gate_pre * (1.0 - sigma))).astype(BF16)
            grad_up = (grad_act * silu_gate).astype(BF16)
            both = jnp.concatenate([grad_gate, grad_up], 1)
            own = jnp.concatenate([contract_rows(mlp_in, both), contract_rows(grad_top, act)], 1).astype(BF16)
            owns.append(own)
            boths.append(both)
            acts.append(act)
            downs.append(three[:, 2 * block :])
            if number < len(mlp_weights) - 1:
                part = contract_cols(both, weight)
                before = part if before is None else before + part
        grad_mlp_in = plane_scatter(
            lambda i, j: contract_cols(both[i:j], weight) + (0.0 if before is None else before[i:j]), own_tokens
        )
        grad_mid_part, mlp_gain_part = norm_back(grad_mlp_in, mid, recip_mlp, mlp_gain, 0)
        grad_mid = out_grad.astype(F32) + grad_mid_part
        mlp_rows = [queue_scatter(own) for own in owns[:-1]]
        grad_mid_b, owns[-1] = after(grad_mid.astype(BF16), owns[-1])
        grad_mid_b = plane_gather(grad_mid_b)
        act = jnp.concatenate(acts, 1)
        act, grad_mid_b = lax.optimization_barrier((act, grad_mid_b))
        down = jnp.concatenate(downs, 1)
        mlp_out = plane_scatter(lambda i, j: contract_cols(act[i:j], down), own_tokens)
        output = (mid + mlp_out).astype(BF16)
        attended_gradient = dot(grad_mid_b, w_o_cols).astype(BF16)
        own_o = contract_rows(grad_mid_b, attended_rows).astype(BF16)
        last_own = jnp.concatenate([owns[-1], own_o], 1)
        mlp_rows.append(queue_scatter(last_own))
        grad_qkv, head_gains = attention_backward(
            proj, *attention, attended_rows, attended_gradient, heads, kv_heads
        )
        own_qkv = contract_rows(normed_rows, grad_qkv).astype(BF16)
        mlp_grads = [hand_out(v) for v in mlp_rows[:-1]] + [None]
        if len(mlp_grads) > 1:
            mlp_grads[0] = both_sides(mlp_grads[0])
        grad_normed = plane_scatter(lambda i, j: contract_cols(grad_qkv[i:j], qkv), own_tokens)
        grad_in_part, attn_gain_part = norm_back(grad_normed, inputs, recip_attn, attn_gain, 0)
        grad_input = grad_mid + grad_in_part
        width = inputs.shape[1]
        sums = sum_everywhere(
            jnp.concatenate([attn_gain_part, mlp_gain_part, head_gains[0], head_gains[1]]).reshape(1, -1), far
        )[0]
        own_qkv, sums, grad_input, mlp_grads[:-1], mlp_rows[-1] = after(
            own_qkv, sums, grad_input, mlp_grads[:-1], mlp_rows[-1]
        )
        qkv_rows = queue_scatter(own_qkv)
        mlp_grads[-1] = hand_out(mlp_rows[-1])
        mlp_grads = [v if isinstance(v, tuple) else both_sides(v) for v in mlp_grads]
        qkv_rows, mlp_grads[1:-1] = after(qkv_rows, mlp_grads[1:-1])
        qkv_pair = both_sides(hand_out(qkv_rows))
        last = len(chunks) - 1
        gate_pieces, up_pieces, down_pieces = ([(j, m * n, n) for j, (_, n) in enumerate(chunks)] for m in range(3))
        grad_w_gate, grad_w_up, grad_w_down, grad_w_o = spread(
            mlp_grads, [gate_pieces, up_pieces, down_pieces, [(last, 3 * chunks[last][1], o_n)]]
        )
        grad_w_q, grad_w_k, grad_w_v = spread([qkv_pair], [[(0, 0, q_n)], [(0, q_n, k_n)], [(0, q_n + k_n, k_n)]])
        return (
            output,
            grad_input,
            grad_w_q,
            grad_w_k,
            grad_w_v,
            grad_w_o,
            grad_w_gate,
            grad_w_up,
            grad_w_down,
            sums[:width],
            sums[width : 2 * width],
            sums[2 * width : 2 * width + head],
            sums[2 * width + head :],
        )

    return on_device


def solution(mesh):
    far = mesh.shape["shard"] // 4
    split = Mesh(mesh.devices.reshape(mesh.shape["rep"], far, 2, 2), ("rep", "far", "mid", "near"))
    tokens = P(("rep", "far", "mid", "near"), None)
    weights = P(("far", "mid", "near"), None)
    return jax.shard_map(
        build(far),
        mesh=split,
        in_specs=(tokens,) * 4 + (P(),) * 4 + (weights,) * 7,
        out_specs=(tokens,) * 2 + (weights,) * 7 + (P(),) * 4,
        check_vma=False,
    )
```

```python
import math

import jax
import jax.numpy as jnp
from jax import lax
from jax.experimental import pallas as pl
from jax.experimental.pallas import tpu as pltpu
from jax.sharding import Mesh
from jax.sharding import PartitionSpec as P

EPSILON = 1e-06
ROPE_BASE = 1000000.0
NEG_FILL = -1e30
F32 = jnp.float32
BF16 = jnp.bfloat16
SWAP = [(0, 1), (1, 0)]


def over_rep(v):
    return lax.ppermute(v, "rep", SWAP)


def over_mid(v):
    return lax.ppermute(v, "mid", SWAP)


def over_near(v):
    return lax.ppermute(v, "near", SWAP)


def plane_gather(own):
    half = own.shape[0] // 2
    from_rep = over_rep(own)
    from_mid = over_mid(own)
    top = over_mid(from_rep[:half])
    bottom = over_rep(from_mid[half:])
    mine = jnp.concatenate([own, from_rep, from_mid, top, bottom], 0)
    return jnp.concatenate([mine, over_near(mine)], 0)


def plane_scatter(partial, rows):
    half = rows // 2
    near = over_near(partial(4 * rows, 8 * rows).astype(BF16))
    part = partial(0, 4 * rows) + near.astype(F32)
    own, rep, mid, both = (part[i * rows : (i + 1) * rows] for i in range(4))
    first_rep = over_rep(jnp.concatenate([both[:half], rep[:half]], 0).astype(BF16))
    first_mid = over_mid(jnp.concatenate([both[half:], mid[half:]], 0).astype(BF16))
    last_mid = over_mid((mid[:half] + first_rep[:half].astype(F32)).astype(BF16))
    last_rep = over_rep((rep[half:] + first_mid[:half].astype(F32)).astype(BF16))
    top = own[:half] + first_rep[half:].astype(F32) + last_mid.astype(F32)
    bottom = own[half:] + last_rep.astype(F32) + first_mid[half:].astype(F32)
    return jnp.concatenate([top, bottom], 0)


def pick_columns(groups):
    side = lax.axis_index("rep").astype(jnp.int32).reshape(1)
    members = [m for group in groups for m in group]
    rows = members[0][0].shape[0]
    widths = [sum(n for _, _, n in group) for group in groups]

    tile = math.gcd(rows, 16)

    def kernel(side_ref, *refs):
        def some(step, carry):
            span = pl.ds(pl.multiple_of(step * tile, tile), tile)
            sources = iter(refs[: len(members)])
            for group, out in zip(groups, refs[len(members) :]):
                at = 0
                for _, _, n in group:
                    source = next(sources)
                    for block in range(4):
                        out[block, span, at : at + n] = source[span, block * n : (block + 1) * n]
                    at += n
            return carry

        lax.fori_loop(0, rows // tile, some, 0)

    def half(start, n):
        return pl.BlockSpec((rows, 4 * n), lambda i, side_ref: (0, start // (4 * n) + side_ref[0]))

    return pl.pallas_call(
        kernel,
        grid_spec=pltpu.PrefetchScalarGridSpec(
            num_scalar_prefetch=1,
            grid=(1,),
            in_specs=[half(start, n) for _, start, n in members],
            out_specs=[pl.BlockSpec((4, rows, w), lambda i, side_ref: (0, 0, 0)) for w in widths],
        ),
        out_shape=[jax.ShapeDtypeStruct((4, rows, w), BF16) for w in widths],
        compiler_params=pltpu.CompilerParams(vmem_limit_bytes=20 << 20),
        name="pick_columns",
    )(side, *[m for m, _, _ in members])


def trade(blocks):
    return lax.all_to_all(blocks, ("mid", "near"), 0, 0)


def gather_rows(blocks):
    four, rows, n = blocks.shape
    return lax.all_gather(blocks.reshape(four * rows, n), "far", axis=0, tiled=True)


def queue_scatter(parts):
    return lax.psum_scatter(parts, "far", scatter_dimension=0, tiled=True)


def hand_out(mine):
    return trade(mine.reshape(4, mine.shape[0] // 4, -1))


def both_sides(mine):
    return (mine, over_rep(mine))


def spread(pairs, outs):
    side = lax.axis_index("rep").astype(jnp.int32).reshape(1)
    rows = pairs[0][0].shape[1]
    columns = [sum(8 * n for _, _, n in pieces) for pieces in outs]

    tile = math.gcd(rows, 16)

    def kernel(side_ref, *refs):
        first = side_ref[0] == 0

        def some(step, carry):
            span = pl.ds(pl.multiple_of(step * tile, tile), tile)
            for out, pieces in zip(refs[2 * len(pairs) :], outs):
                at = 0
                for pair, start, n in pieces:
                    own, other = refs[2 * pair], refs[2 * pair + 1]
                    for block in range(4):
                        a = own[block, span, start : start + n].astype(F32)
                        b = other[block, span, start : start + n].astype(F32)
                        out[span, at + block * n : at + (block + 1) * n] = jnp.where(first, a, b)
                        out[span, at + (4 + block) * n : at + (5 + block) * n] = jnp.where(first, b, a)
                    at += 8 * n
            return carry

        lax.fori_loop(0, rows // tile, some, 0)

    return pl.pallas_call(
        kernel,
        in_specs=[pl.BlockSpec(memory_space=pltpu.SMEM)] + [pl.BlockSpec(memory_space=pltpu.VMEM)] * (2 * len(pairs)),
        out_specs=[pl.BlockSpec(memory_space=pltpu.VMEM)] * len(outs),
        out_shape=[jax.ShapeDtypeStruct((rows, c), F32) for c in columns],
        compiler_params=pltpu.CompilerParams(vmem_limit_bytes=40 << 20),
        name="spread",
    )(side, *[v for pair in pairs for v in pair])


def sum_everywhere(v, size):
    for axis in ("near", "mid", "rep"):
        v = v + lax.ppermute(v, axis, SWAP)
    if size & (size - 1):
        return lax.psum(v, "far")
    step = 1
    while step < size:
        v = v + lax.ppermute(v, "far", [(i, i ^ step) for i in range(size)])
        step *= 2
    return v


def after(*values):
    return lax.optimization_barrier(values)


def rope_tables(positions, half):
    freq = jnp.exp(jnp.arange(half, dtype=F32) * (-math.log(ROPE_BASE) / half))
    angles = positions.reshape(-1).astype(F32)[:, None] * freq
    cosine, sine = (jnp.cos(angles), jnp.sin(angles))
    return (jnp.concatenate([cosine, cosine], 1), jnp.concatenate([-sine, sine], 1))


def norm_back(grads, inputs, recip, gain, axes):
    normal = inputs * recip
    scaled = grads * gain
    gain_grad = jnp.sum(grads * normal, axis=axes)
    input_grad = recip * (scaled - normal * jnp.mean(scaled * normal, -1, keepdims=True))
    return (input_grad, gain_grad)


def dot(left, right):
    return jnp.dot(left, right, preferred_element_type=F32)


def contract_rows(left, right):
    return lax.dot_general(left, right, (((0,), (0,)), ((), ())), preferred_element_type=F32)


def contract_cols(left, right):
    return lax.dot_general(left, right, (((1,), (1,)), ((), ())), preferred_element_type=F32)


def swap_halves(v):
    half = v.shape[-1] // 2
    return jnp.concatenate([v[:, half:], v[:, :half]], -1)


def unit(u):
    recip = lax.rsqrt(jnp.mean(u * u, -1, keepdims=True) + EPSILON)
    return (u * recip, recip)


def sequence_state(proj_ref, cosine_ref, sine_ref, down_ref, across_ref, head):
    length = proj_ref.shape[0]
    later = lax.broadcasted_iota(jnp.int32, (length, length), 0)
    earlier = lax.broadcasted_iota(jnp.int32, (length, length), 1)
    mask = (down_ref[...] == across_ref[0]) & (earlier <= later)
    cosine, sine = cosine_ref[...], sine_ref[...]

    def turned(v):
        return v * cosine + swap_halves(v) * sine

    def turned_back(v):
        return v * cosine - swap_halves(v) * sine

    def columns(i):
        return proj_ref[:, i * head : (i + 1) * head]

    return (mask, turned, turned_back, columns)


def masked_scores(query, key, mask, head):
    return jnp.where(mask, contract_cols(query, key) * head ** (-0.5), NEG_FILL)


def attention_forward(proj, cosine, sine, down, across, q_gain, k_gain, heads, kv_heads):
    head = q_gain.shape[1]
    sequences, _, length = across.shape
    groups = heads // kv_heads

    def kernel(proj_ref, cosine_ref, sine_ref, down_ref, across_ref, q_gain_ref, k_gain_ref, out_ref):
        mask, turned, _, columns = sequence_state(proj_ref, cosine_ref, sine_ref, down_ref, across_ref, head)
        for kv in range(kv_heads):
            key = turned(unit(columns(heads + kv))[0] * k_gain_ref[...]).astype(BF16)
            value = columns(heads + kv_heads + kv).astype(BF16)
            for h in range(kv * groups, (kv + 1) * groups):
                query = turned(unit(columns(h))[0] * q_gain_ref[...]).astype(BF16)
                scores = masked_scores(query, key, mask, head)
                expo = jnp.exp(scores - jnp.max(scores, -1, keepdims=True))
                probs = (expo / jnp.sum(expo, -1, keepdims=True)).astype(BF16)
                out_ref[:, h * head : (h + 1) * head] = dot(probs, value).astype(BF16)

    row = lambda n: pl.BlockSpec((length, n), lambda i: (i, 0))
    fixed = pl.BlockSpec((1, head), lambda i: (0, 0))
    return pl.pallas_call(
        kernel,
        grid=(sequences,),
        in_specs=[row(proj.shape[1]), row(head), row(head), row(1)]
        + [pl.BlockSpec((1, 1, length), lambda i: (i, 0, 0)), fixed, fixed],
        out_specs=row(heads * head),
        out_shape=jax.ShapeDtypeStruct((proj.shape[0], heads * head), BF16),
        compiler_params=pltpu.CompilerParams(vmem_limit_bytes=6 << 20),
        name="attention_forward",
    )(proj, cosine, sine, down, across, q_gain, k_gain)


def attention_backward(proj, cosine, sine, down, across, q_gain, k_gain, attended, attended_grad, heads, kv_heads):
    head = q_gain.shape[1]
    sequences, _, length = across.shape
    groups = heads // kv_heads
    scale = head ** (-0.5)

    def kernel(
        proj_ref,
        cosine_ref,
        sine_ref,
        down_ref,
        across_ref,
        q_gain_ref,
        k_gain_ref,
        attended_ref,
        grad_ref,
        out_ref,
        gains_ref,
    ):
        mask, turned, turned_back, columns = sequence_state(
            proj_ref, cosine_ref, sine_ref, down_ref, across_ref, head
        )

        @pl.when(pl.program_id(0) == 0)
        def _():
            gains_ref[...] = jnp.zeros_like(gains_ref)

        def put(i, v):
            out_ref[:, i * head : (i + 1) * head] = v.astype(BF16)

        def norm_grad(i, grads, normal, recip, gain, row):
            scaled = grads * gain
            gains_ref[row : row + 1, :] += jnp.sum(grads * normal, 0, keepdims=True)
            put(i, recip * (scaled - normal * jnp.mean(scaled * normal, -1, keepdims=True)))

        for kv in range(kv_heads):
            key_unit, key_recip = unit(columns(heads + kv))
            key = turned(key_unit * k_gain_ref[...]).astype(BF16)
            value = columns(heads + kv_heads + kv).astype(BF16)
            grad_value = jnp.zeros((length, head), F32)
            grad_key = jnp.zeros((length, head), F32)
            for h in range(kv * groups, (kv + 1) * groups):
                query_unit, query_recip = unit(columns(h))
                query = turned(query_unit * q_gain_ref[...]).astype(BF16)
                scores = masked_scores(query, key, mask, head)
                top = jnp.max(scores, -1, keepdims=True)
                log_total = top + jnp.log(jnp.sum(jnp.exp(scores - top), -1, keepdims=True))
                probs = jnp.where(mask, jnp.exp(scores - log_total), 0.0)
                grad = grad_ref[:, h * head : (h + 1) * head]
                grad_value += contract_rows(probs.astype(BF16), grad)
                complete = attended_ref[:, h * head : (h + 1) * head].astype(F32)
                delta = jnp.sum(grad.astype(F32) * complete, -1, keepdims=True)
                grad_scores = (probs * (contract_cols(grad, value) - delta)).astype(BF16)
                grad_query = dot(grad_scores, key) * scale
                grad_key += contract_rows(grad_scores, query)
                norm_grad(h, turned_back(grad_query), query_unit, query_recip, q_gain_ref[...], 0)
            norm_grad(heads + kv, turned_back(grad_key * scale), key_unit, key_recip, k_gain_ref[...], 1)
            put(heads + kv_heads + kv, grad_value)

    row = lambda n: pl.BlockSpec((length, n), lambda i: (i, 0))
    fixed = pl.BlockSpec((1, head), lambda i: (0, 0))
    return pl.pallas_call(
        kernel,
        grid=(sequences,),
        in_specs=[row(proj.shape[1]), row(head), row(head), row(1)]
        + [pl.BlockSpec((1, 1, length), lambda i: (i, 0, 0)), fixed, fixed]
        + [row(heads * head), row(heads * head)],
        out_specs=[row(proj.shape[1]), pl.BlockSpec((8, head), lambda i: (0, 0))],
        out_shape=[jax.ShapeDtypeStruct(proj.shape, BF16), jax.ShapeDtypeStruct((8, head), F32)],
        compiler_params=pltpu.CompilerParams(vmem_limit_bytes=8 << 20),
        name="attention_backward",
    )(proj, cosine, sine, down, across, q_gain, k_gain, attended, attended_grad)


def plane_notes(own):
    pair = jnp.concatenate([own, over_near(own)], 0)
    four = jnp.concatenate([pair, over_mid(pair)], 0)
    eight = jnp.concatenate([four, over_rep(four)], 0)
    return jnp.concatenate([eight[i : i + 1] for i in (0, 4, 2, 6, 1, 5, 3, 7)], 0)


def build(far):
    def on_device(
        block_input,
        out_grad,
        segments,
        positions,
        attn_gain,
        mlp_gain,
        q_gain,
        k_gain,
        w_q,
        key_matrix,
        value_matrix,
        w_o,
        w_gate,
        w_up,
        w_down,
    ):
        head = q_gain.shape[0]
        heads = w_q.shape[1] // head // 8
        kv_heads = key_matrix.shape[1] // head // 8
        hidden = w_gate.shape[1]
        rows = w_q.shape[0]
        q_cols = heads * head
        k_cols = kv_heads * head
        part = hidden // 3 if hidden % 3072 == 0 else hidden
        chunks = [(start, part // 8) for start in range(0, hidden, part)]

        q_n, k_n, o_n = (w.shape[1] // 8 for w in (w_q, key_matrix, w_o))
        (attn_slot,) = pick_columns(
            [[(w_q, 0, q_n), (key_matrix, 0, k_n), (value_matrix, 0, k_n), (w_o, 0, o_n)]]
        )
        mlp_slots = pick_columns(
            [[(w, start, n) for start, n in part for w in (w_gate, w_up, w_down)] for part in (chunks[:-1], chunks[-1:]) if part]
        )
        inputs = block_input.astype(F32)
        recip_attn = lax.rsqrt(jnp.mean(inputs * inputs, -1, keepdims=True) + EPSILON)
        normed_own = (inputs * recip_attn * attn_gain).astype(BF16)
        traded = [trade(slot) for slot in (attn_slot, *mlp_slots)]
        attn_weights, *gathered = [gather_rows(v) for v in traded]
        mlp_weights = []
        for part in gathered:
            step = 3 * chunks[0][1]
            mlp_weights += [part[:, at : at + step] for at in range(0, part.shape[1], step)]
        qkv, w_o_cols = attn_weights[:, : q_n + 2 * k_n], attn_weights[:, q_n + 2 * k_n :]

        normed_rows = plane_gather(normed_own)
        grad_top = plane_gather(out_grad)
        notes = plane_notes(jnp.concatenate([segments, positions], 1))
        length = segments.shape[1]
        own_tokens = inputs.shape[0]
        tokens = normed_rows.shape[0]
        across = notes[:, None, :length]
        cosine, sine = rope_tables(notes[:, length:], head // 2)
        attention = (cosine, sine, across.reshape(tokens, 1), across, q_gain[None], k_gain[None])

        proj = dot(normed_rows, qkv)
        attended_rows = attention_forward(proj, *attention, heads, kv_heads)
        attended_rows, grad_top = lax.optimization_barrier((attended_rows, grad_top))
        mid = inputs + plane_scatter(lambda i, j: contract_cols(attended_rows[i:j], w_o_cols), own_tokens)
        recip_mlp = lax.rsqrt(jnp.mean(mid * mid, -1, keepdims=True) + EPSILON)
        mlp_in = plane_gather((mid * recip_mlp * mlp_gain).astype(BF16))

        acts, downs, owns, boths = [], [], [], []
        before = None
        for number, three in enumerate(mlp_weights):
            block = chunks[number][1]
            if number == 2:
                three, owns[0] = after(three, owns[0])
            weight = three[:, : 2 * block]
            pre = dot(mlp_in, weight)
            gate_pre, up_pre = pre[:, :block], pre[:, block:]
            sigma = jax.nn.sigmoid(gate_pre)
            silu_gate = gate_pre * sigma
            act = (silu_gate * up_pre).astype(BF16)
            grad_act = dot(grad_top, three[:, 2 * block :])
            grad_gate = (grad_act * up_pre * sigma * (1.0 + gate_pre * (1.0 - sigma))).astype(BF16)
            grad_up = (grad_act * silu_gate).astype(BF16)
            both = jnp.concatenate([grad_gate, grad_up], 1)
            own = jnp.concatenate([contract_rows(mlp_in, both), contract_rows(grad_top, act)], 1).astype(BF16)
            owns.append(own)
            boths.append(both)
            acts.append(act)
            downs.append(three[:, 2 * block :])
            if number < len(mlp_weights) - 1:
                part = contract_cols(both, weight)
                before = part if before is None else before + part
        grad_mlp_in = plane_scatter(
            lambda i, j: contract_cols(both[i:j], weight) + (0.0 if before is None else before[i:j]), own_tokens
        )
        grad_mid_part, mlp_gain_part = norm_back(grad_mlp_in, mid, recip_mlp, mlp_gain, 0)
        grad_mid = out_grad.astype(F32) + grad_mid_part
        mlp_rows = [queue_scatter(own) for own in owns[:-1]]
        grad_mid_b, owns[-1] = after(grad_mid.astype(BF16), owns[-1])
        grad_mid_b = plane_gather(grad_mid_b)
        act = jnp.concatenate(acts, 1)
        attended_gradient = dot(grad_mid_b, w_o_cols).astype(BF16)
        own_o = contract_rows(grad_mid_b, attended_rows).astype(BF16)
        last_own = jnp.concatenate([owns[-1], own_o], 1)
        mlp_rows.append(queue_scatter(last_own))
        grad_qkv, head_gains = attention_backward(
            proj, *attention, attended_rows, attended_gradient, heads, kv_heads
        )
        own_qkv = contract_rows(normed_rows, grad_qkv).astype(BF16)
        mlp_grads = [hand_out(v) for v in mlp_rows[:-1]] + [None]
        if len(mlp_grads) > 1:
            mlp_grads[0] = both_sides(mlp_grads[0])
        grad_normed = plane_scatter(lambda i, j: contract_cols(grad_qkv[i:j], qkv), own_tokens)
        grad_in_part, attn_gain_part = norm_back(grad_normed, inputs, recip_attn, attn_gain, 0)
        grad_input = grad_mid + grad_in_part
        width = inputs.shape[1]
        sums = sum_everywhere(
            jnp.concatenate([attn_gain_part, mlp_gain_part, head_gains[0], head_gains[1]]).reshape(1, -1), far
        )[0]
        own_qkv, sums, grad_input, mlp_grads[:-1], mlp_rows[-1] = after(
            own_qkv, sums, grad_input, mlp_grads[:-1], mlp_rows[-1]
        )
        qkv_rows = queue_scatter(own_qkv)
        mlp_grads[-1] = hand_out(mlp_rows[-1])
        act, mlp_grads[-1] = after(act, mlp_grads[-1])
        down = jnp.concatenate(downs, 1)
        mlp_out = plane_scatter(lambda i, j: contract_cols(act[i:j], down), own_tokens)
        output = (mid + mlp_out).astype(BF16)
        mlp_grads = [v if isinstance(v, tuple) else both_sides(v) for v in mlp_grads]
        qkv_rows, mlp_grads[1:-1] = after(qkv_rows, mlp_grads[1:-1])
        qkv_pair = both_sides(hand_out(qkv_rows))
        last = len(chunks) - 1
        gate_pieces, up_pieces, down_pieces = ([(j, m * n, n) for j, (_, n) in enumerate(chunks)] for m in range(3))
        grad_w_gate, grad_w_up, grad_w_down, grad_w_o = spread(
            mlp_grads, [gate_pieces, up_pieces, down_pieces, [(last, 3 * chunks[last][1], o_n)]]
        )
        grad_w_q, grad_w_k, grad_w_v = spread([qkv_pair], [[(0, 0, q_n)], [(0, q_n, k_n)], [(0, q_n + k_n, k_n)]])
        return (
            output,
            grad_input,
            grad_w_q,
            grad_w_k,
            grad_w_v,
            grad_w_o,
            grad_w_gate,
            grad_w_up,
            grad_w_down,
            sums[:width],
            sums[width : 2 * width],
            sums[2 * width : 2 * width + head],
            sums[2 * width + head :],
        )

    return on_device


def solution(mesh):
    far = mesh.shape["shard"] // 4
    split = Mesh(mesh.devices.reshape(mesh.shape["rep"], far, 2, 2), ("rep", "far", "mid", "near"))
    tokens = P(("rep", "far", "mid", "near"), None)
    weights = P(("far", "mid", "near"), None)
    return jax.shard_map(
        build(far),
        mesh=split,
        in_specs=(tokens,) * 4 + (P(),) * 4 + (weights,) * 7,
        out_specs=(tokens,) * 2 + (weights,) * 7 + (P(),) * 4,
        check_vma=False,
    )
```

```python
import math

import jax
import jax.numpy as jnp
from jax import lax
from jax.experimental import pallas as pl
from jax.experimental.pallas import tpu as pltpu
from jax.sharding import Mesh
from jax.sharding import PartitionSpec as P

EPSILON = 1e-06
ROPE_BASE = 1000000.0
NEG_FILL = -1e30
F32 = jnp.float32
BF16 = jnp.bfloat16
SWAP = [(0, 1), (1, 0)]


def over_rep(v):
    return lax.ppermute(v, "rep", SWAP)


def over_mid(v):
    return lax.ppermute(v, "mid", SWAP)


def over_near(v):
    return lax.ppermute(v, "near", SWAP)


def plane_gather(own):
    half = own.shape[0] // 2
    from_rep = over_rep(own)
    from_mid = over_mid(own)
    top = over_mid(from_rep[:half])
    bottom = over_rep(from_mid[half:])
    mine = jnp.concatenate([own, from_rep, from_mid, top, bottom], 0)
    return jnp.concatenate([mine, over_near(mine)], 0)


def plane_scatter(partial, rows):
    half = rows // 2
    near = over_near(partial(4 * rows, 8 * rows).astype(BF16))
    part = partial(0, 4 * rows) + near.astype(F32)
    own, rep, mid, both = (part[i * rows : (i + 1) * rows] for i in range(4))
    first_rep = over_rep(jnp.concatenate([both[:half], rep[:half]], 0).astype(BF16))
    first_mid = over_mid(jnp.concatenate([both[half:], mid[half:]], 0).astype(BF16))
    last_mid = over_mid((mid[:half] + first_rep[:half].astype(F32)).astype(BF16))
    last_rep = over_rep((rep[half:] + first_mid[:half].astype(F32)).astype(BF16))
    top = own[:half] + first_rep[half:].astype(F32) + last_mid.astype(F32)
    bottom = own[half:] + last_rep.astype(F32) + first_mid[half:].astype(F32)
    return jnp.concatenate([top, bottom], 0)


def pick_columns(groups):
    side = lax.axis_index("rep").astype(jnp.int32).reshape(1)
    members = [m for group in groups for m in group]
    rows = members[0][0].shape[0]
    widths = [sum(n for _, _, n in group) for group in groups]

    tile = math.gcd(rows, 16)

    def kernel(side_ref, *refs):
        def some(step, carry):
            span = pl.ds(pl.multiple_of(step * tile, tile), tile)
            sources = iter(refs[: len(members)])
            for group, out in zip(groups, refs[len(members) :]):
                at = 0
                for _, _, n in group:
                    source = next(sources)
                    for block in range(4):
                        out[block, span, at : at + n] = source[span, block * n : (block + 1) * n]
                    at += n
            return carry

        lax.fori_loop(0, rows // tile, some, 0)

    def half(start, n):
        return pl.BlockSpec((rows, 4 * n), lambda i, side_ref: (0, start // (4 * n) + side_ref[0]))

    return pl.pallas_call(
        kernel,
        grid_spec=pltpu.PrefetchScalarGridSpec(
            num_scalar_prefetch=1,
            grid=(1,),
            in_specs=[half(start, n) for _, start, n in members],
            out_specs=[pl.BlockSpec((4, rows, w), lambda i, side_ref: (0, 0, 0)) for w in widths],
        ),
        out_shape=[jax.ShapeDtypeStruct((4, rows, w), BF16) for w in widths],
        compiler_params=pltpu.CompilerParams(vmem_limit_bytes=20 << 20),
        name="pick_columns",
    )(side, *[m for m, _, _ in members])


def trade(blocks):
    return lax.all_to_all(blocks, ("mid", "near"), 0, 0)


def gather_rows(blocks):
    four, rows, n = blocks.shape
    return lax.all_gather(blocks.reshape(four * rows, n), "far", axis=0, tiled=True)


def queue_scatter(parts):
    return lax.psum_scatter(parts, "far", scatter_dimension=0, tiled=True)


def hand_out(mine):
    return trade(mine.reshape(4, mine.shape[0] // 4, -1))


def both_sides(mine):
    return (mine, over_rep(mine))


def spread(pairs, outs):
    side = lax.axis_index("rep").astype(jnp.int32).reshape(1)
    rows = pairs[0][0].shape[1]
    columns = [sum(8 * n for _, _, n in pieces) for pieces in outs]

    tile = math.gcd(rows, 16)

    def kernel(side_ref, *refs):
        first = side_ref[0] == 0

        def some(step, carry):
            span = pl.ds(pl.multiple_of(step * tile, tile), tile)
            for out, pieces in zip(refs[2 * len(pairs) :], outs):
                at = 0
                for pair, start, n in pieces:
                    own, other = refs[2 * pair], refs[2 * pair + 1]
                    for block in range(4):
                        a = own[block, span, start : start + n].astype(F32)
                        b = other[block, span, start : start + n].astype(F32)
                        out[span, at + block * n : at + (block + 1) * n] = jnp.where(first, a, b)
                        out[span, at + (4 + block) * n : at + (5 + block) * n] = jnp.where(first, b, a)
                    at += 8 * n
            return carry

        lax.fori_loop(0, rows // tile, some, 0)

    return pl.pallas_call(
        kernel,
        in_specs=[pl.BlockSpec(memory_space=pltpu.SMEM)] + [pl.BlockSpec(memory_space=pltpu.VMEM)] * (2 * len(pairs)),
        out_specs=[pl.BlockSpec(memory_space=pltpu.VMEM)] * len(outs),
        out_shape=[jax.ShapeDtypeStruct((rows, c), F32) for c in columns],
        compiler_params=pltpu.CompilerParams(vmem_limit_bytes=40 << 20),
        name="spread",
    )(side, *[v for pair in pairs for v in pair])


def sum_everywhere(v, size):
    for axis in ("near", "mid", "rep"):
        v = v + lax.ppermute(v, axis, SWAP)
    if size & (size - 1):
        return lax.psum(v, "far")
    step = 1
    while step < size:
        v = v + lax.ppermute(v, "far", [(i, i ^ step) for i in range(size)])
        step *= 2
    return v


def after(*values):
    return lax.optimization_barrier(values)


def rope_tables(positions, half):
    freq = jnp.exp(jnp.arange(half, dtype=F32) * (-math.log(ROPE_BASE) / half))
    angles = positions.reshape(-1).astype(F32)[:, None] * freq
    cosine, sine = (jnp.cos(angles), jnp.sin(angles))
    return (jnp.concatenate([cosine, cosine], 1), jnp.concatenate([-sine, sine], 1))


def norm_back(grads, inputs, recip, gain, axes):
    normal = inputs * recip
    scaled = grads * gain
    gain_grad = jnp.sum(grads * normal, axis=axes)
    input_grad = recip * (scaled - normal * jnp.mean(scaled * normal, -1, keepdims=True))
    return (input_grad, gain_grad)


def dot(left, right):
    return jnp.dot(left, right, preferred_element_type=F32)


def contract_rows(left, right):
    return lax.dot_general(left, right, (((0,), (0,)), ((), ())), preferred_element_type=F32)


def contract_cols(left, right):
    return lax.dot_general(left, right, (((1,), (1,)), ((), ())), preferred_element_type=F32)


def swap_halves(v):
    half = v.shape[-1] // 2
    return jnp.concatenate([v[:, half:], v[:, :half]], -1)


def unit(u):
    recip = lax.rsqrt(jnp.mean(u * u, -1, keepdims=True) + EPSILON)
    return (u * recip, recip)


def sequence_state(proj_ref, cosine_ref, sine_ref, down_ref, across_ref, head):
    length = proj_ref.shape[0]
    later = lax.broadcasted_iota(jnp.int32, (length, length), 0)
    earlier = lax.broadcasted_iota(jnp.int32, (length, length), 1)
    mask = (down_ref[...] == across_ref[0]) & (earlier <= later)
    cosine, sine = cosine_ref[...], sine_ref[...]

    def turned(v):
        return v * cosine + swap_halves(v) * sine

    def turned_back(v):
        return v * cosine - swap_halves(v) * sine

    def columns(i):
        return proj_ref[:, i * head : (i + 1) * head]

    return (mask, turned, turned_back, columns)


def masked_scores(query, key, mask, head):
    return jnp.where(mask, contract_cols(query, key) * head ** (-0.5), NEG_FILL)


def attention_forward(proj, cosine, sine, down, across, q_gain, k_gain, heads, kv_heads):
    head = q_gain.shape[1]
    sequences, _, length = across.shape
    groups = heads // kv_heads

    def kernel(proj_ref, cosine_ref, sine_ref, down_ref, across_ref, q_gain_ref, k_gain_ref, out_ref):
        mask, turned, _, columns = sequence_state(proj_ref, cosine_ref, sine_ref, down_ref, across_ref, head)
        for kv in range(kv_heads):
            key = turned(unit(columns(heads + kv))[0] * k_gain_ref[...]).astype(BF16)
            value = columns(heads + kv_heads + kv).astype(BF16)
            for h in range(kv * groups, (kv + 1) * groups):
                query = turned(unit(columns(h))[0] * q_gain_ref[...]).astype(BF16)
                scores = masked_scores(query, key, mask, head)
                expo = jnp.exp(scores - jnp.max(scores, -1, keepdims=True))
                probs = (expo / jnp.sum(expo, -1, keepdims=True)).astype(BF16)
                out_ref[:, h * head : (h + 1) * head] = dot(probs, value).astype(BF16)

    row = lambda n: pl.BlockSpec((length, n), lambda i: (i, 0))
    fixed = pl.BlockSpec((1, head), lambda i: (0, 0))
    return pl.pallas_call(
        kernel,
        grid=(sequences,),
        in_specs=[row(proj.shape[1]), row(head), row(head), row(1)]
        + [pl.BlockSpec((1, 1, length), lambda i: (i, 0, 0)), fixed, fixed],
        out_specs=row(heads * head),
        out_shape=jax.ShapeDtypeStruct((proj.shape[0], heads * head), BF16),
        compiler_params=pltpu.CompilerParams(vmem_limit_bytes=6 << 20),
        name="attention_forward",
    )(proj, cosine, sine, down, across, q_gain, k_gain)


def attention_backward(proj, cosine, sine, down, across, q_gain, k_gain, attended, attended_grad, heads, kv_heads):
    head = q_gain.shape[1]
    sequences, _, length = across.shape
    groups = heads // kv_heads
    scale = head ** (-0.5)

    def kernel(
        proj_ref,
        cosine_ref,
        sine_ref,
        down_ref,
        across_ref,
        q_gain_ref,
        k_gain_ref,
        attended_ref,
        grad_ref,
        out_ref,
        gains_ref,
    ):
        mask, turned, turned_back, columns = sequence_state(
            proj_ref, cosine_ref, sine_ref, down_ref, across_ref, head
        )

        @pl.when(pl.program_id(0) == 0)
        def _():
            gains_ref[...] = jnp.zeros_like(gains_ref)

        def put(i, v):
            out_ref[:, i * head : (i + 1) * head] = v.astype(BF16)

        def norm_grad(i, grads, normal, recip, gain, row):
            scaled = grads * gain
            gains_ref[row : row + 1, :] += jnp.sum(grads * normal, 0, keepdims=True)
            put(i, recip * (scaled - normal * jnp.mean(scaled * normal, -1, keepdims=True)))

        for kv in range(kv_heads):
            key_unit, key_recip = unit(columns(heads + kv))
            key = turned(key_unit * k_gain_ref[...]).astype(BF16)
            value = columns(heads + kv_heads + kv).astype(BF16)
            grad_value = jnp.zeros((length, head), F32)
            grad_key = jnp.zeros((length, head), F32)
            for h in range(kv * groups, (kv + 1) * groups):
                query_unit, query_recip = unit(columns(h))
                query = turned(query_unit * q_gain_ref[...]).astype(BF16)
                scores = masked_scores(query, key, mask, head)
                top = jnp.max(scores, -1, keepdims=True)
                log_total = top + jnp.log(jnp.sum(jnp.exp(scores - top), -1, keepdims=True))
                probs = jnp.where(mask, jnp.exp(scores - log_total), 0.0)
                grad = grad_ref[:, h * head : (h + 1) * head]
                grad_value += contract_rows(probs.astype(BF16), grad)
                complete = attended_ref[:, h * head : (h + 1) * head].astype(F32)
                delta = jnp.sum(grad.astype(F32) * complete, -1, keepdims=True)
                grad_scores = (probs * (contract_cols(grad, value) - delta)).astype(BF16)
                grad_query = dot(grad_scores, key) * scale
                grad_key += contract_rows(grad_scores, query)
                norm_grad(h, turned_back(grad_query), query_unit, query_recip, q_gain_ref[...], 0)
            norm_grad(heads + kv, turned_back(grad_key * scale), key_unit, key_recip, k_gain_ref[...], 1)
            put(heads + kv_heads + kv, grad_value)

    row = lambda n: pl.BlockSpec((length, n), lambda i: (i, 0))
    fixed = pl.BlockSpec((1, head), lambda i: (0, 0))
    return pl.pallas_call(
        kernel,
        grid=(sequences,),
        in_specs=[row(proj.shape[1]), row(head), row(head), row(1)]
        + [pl.BlockSpec((1, 1, length), lambda i: (i, 0, 0)), fixed, fixed]
        + [row(heads * head), row(heads * head)],
        out_specs=[row(proj.shape[1]), pl.BlockSpec((8, head), lambda i: (0, 0))],
        out_shape=[jax.ShapeDtypeStruct(proj.shape, BF16), jax.ShapeDtypeStruct((8, head), F32)],
        compiler_params=pltpu.CompilerParams(vmem_limit_bytes=8 << 20),
        name="attention_backward",
    )(proj, cosine, sine, down, across, q_gain, k_gain, attended, attended_grad)


def plane_notes(own):
    pair = jnp.concatenate([own, over_near(own)], 0)
    four = jnp.concatenate([pair, over_mid(pair)], 0)
    eight = jnp.concatenate([four, over_rep(four)], 0)
    return jnp.concatenate([eight[i : i + 1] for i in (0, 4, 2, 6, 1, 5, 3, 7)], 0)


def build(far):
    def on_device(
        block_input,
        out_grad,
        segments,
        positions,
        attn_gain,
        mlp_gain,
        q_gain,
        k_gain,
        w_q,
        key_matrix,
        value_matrix,
        w_o,
        w_gate,
        w_up,
        w_down,
    ):
        head = q_gain.shape[0]
        heads = w_q.shape[1] // head // 8
        kv_heads = key_matrix.shape[1] // head // 8
        hidden = w_gate.shape[1]
        rows = w_q.shape[0]
        q_cols = heads * head
        k_cols = kv_heads * head
        part = hidden // 3 if hidden % 3072 == 0 else hidden
        chunks = [(start, part // 8) for start in range(0, hidden, part)]

        q_n, k_n, o_n = (w.shape[1] // 8 for w in (w_q, key_matrix, w_o))
        (attn_slot,) = pick_columns(
            [[(w_q, 0, q_n), (key_matrix, 0, k_n), (value_matrix, 0, k_n), (w_o, 0, o_n)]]
        )
        mlp_slots = pick_columns(
            [[(w, start, n) for start, n in part for w in (w_gate, w_up, w_down)] for part in (chunks[:-1], chunks[-1:]) if part]
        )
        inputs = block_input.astype(F32)
        recip_attn = lax.rsqrt(jnp.mean(inputs * inputs, -1, keepdims=True) + EPSILON)
        normed_own = (inputs * recip_attn * attn_gain).astype(BF16)
        traded = [trade(slot) for slot in (attn_slot, *mlp_slots)]
        attn_weights, *gathered = [gather_rows(v) for v in traded]
        mlp_weights = []
        for part in gathered:
            step = 3 * chunks[0][1]
            mlp_weights += [part[:, at : at + step] for at in range(0, part.shape[1], step)]
        qkv, w_o_cols = attn_weights[:, : q_n + 2 * k_n], attn_weights[:, q_n + 2 * k_n :]

        normed_rows = plane_gather(normed_own)
        grad_top = plane_gather(out_grad)
        notes = plane_notes(jnp.concatenate([segments, positions], 1))
        length = segments.shape[1]
        own_tokens = inputs.shape[0]
        tokens = normed_rows.shape[0]
        across = notes[:, None, :length]
        cosine, sine = rope_tables(notes[:, length:], head // 2)
        attention = (cosine, sine, across.reshape(tokens, 1), across, q_gain[None], k_gain[None])

        proj = dot(normed_rows, qkv)
        attended_rows = attention_forward(proj, *attention, heads, kv_heads)
        attended_rows, grad_top = lax.optimization_barrier((attended_rows, grad_top))
        mid = inputs + plane_scatter(lambda i, j: contract_cols(attended_rows[i:j], w_o_cols), own_tokens)
        recip_mlp = lax.rsqrt(jnp.mean(mid * mid, -1, keepdims=True) + EPSILON)
        mlp_in = plane_gather((mid * recip_mlp * mlp_gain).astype(BF16))

        acts, downs, owns, boths = [], [], [], []
        before = None
        for number, three in enumerate(mlp_weights):
            block = chunks[number][1]
            if number == 2:
                three, owns[0], acts[-1] = after(three, owns[0], acts[-1])
            weight = three[:, : 2 * block]
            pre = dot(mlp_in, weight)
            gate_pre, up_pre = pre[:, :block], pre[:, block:]
            sigma = jax.nn.sigmoid(gate_pre)
            silu_gate = gate_pre * sigma
            act = (silu_gate * up_pre).astype(BF16)
            grad_act = dot(grad_top, three[:, 2 * block :])
            grad_gate = (grad_act * up_pre * sigma * (1.0 + gate_pre * (1.0 - sigma))).astype(BF16)
            grad_up = (grad_act * silu_gate).astype(BF16)
            both = jnp.concatenate([grad_gate, grad_up], 1)
            own = jnp.concatenate([contract_rows(mlp_in, both), contract_rows(grad_top, act)], 1).astype(BF16)
            owns.append(own)
            boths.append(both)
            acts.append(act)
            downs.append(three[:, 2 * block :])
            if number < len(mlp_weights) - 1:
                part = contract_cols(both, weight)
                before = part if before is None else before + part
        grad_mlp_in = plane_scatter(
            lambda i, j: contract_cols(both[i:j], weight) + (0.0 if before is None else before[i:j]), own_tokens
        )
        grad_mid_part, mlp_gain_part = norm_back(grad_mlp_in, mid, recip_mlp, mlp_gain, 0)
        grad_mid = out_grad.astype(F32) + grad_mid_part
        mlp_rows = [queue_scatter(own) for own in owns[:-1]]
        grad_mid_b, owns[-1] = after(grad_mid.astype(BF16), owns[-1])
        grad_mid_b = plane_gather(grad_mid_b)
        act = jnp.concatenate(acts, 1)
        act, grad_mid_b = lax.optimization_barrier((act, grad_mid_b))
        down = jnp.concatenate(downs, 1)
        mlp_out = plane_scatter(lambda i, j: contract_cols(act[i:j], down), own_tokens)
        output = (mid + mlp_out).astype(BF16)
        attended_gradient = dot(grad_mid_b, w_o_cols).astype(BF16)
        own_o = contract_rows(grad_mid_b, attended_rows).astype(BF16)
        last_own = jnp.concatenate([owns[-1], own_o], 1)
        mlp_rows.append(queue_scatter(last_own))
        grad_qkv, head_gains = attention_backward(
            proj, *attention, attended_rows, attended_gradient, heads, kv_heads
        )
        own_qkv = contract_rows(normed_rows, grad_qkv).astype(BF16)
        mlp_grads = [hand_out(v) for v in mlp_rows[:-1]] + [None]
        if len(mlp_grads) > 1:
            mlp_grads[0] = both_sides(mlp_grads[0])
        grad_normed = plane_scatter(lambda i, j: contract_cols(grad_qkv[i:j], qkv), own_tokens)
        grad_in_part, attn_gain_part = norm_back(grad_normed, inputs, recip_attn, attn_gain, 0)
        grad_input = grad_mid + grad_in_part
        width = inputs.shape[1]
        sums = sum_everywhere(
            jnp.concatenate([attn_gain_part, mlp_gain_part, head_gains[0], head_gains[1]]).reshape(1, -1), far
        )[0]
        own_qkv, sums, grad_input, mlp_grads[:-1], mlp_rows[-1] = after(
            own_qkv, sums, grad_input, mlp_grads[:-1], mlp_rows[-1]
        )
        qkv_rows = queue_scatter(own_qkv)
        mlp_grads[-1] = hand_out(mlp_rows[-1])
        mlp_grads = [v if isinstance(v, tuple) else both_sides(v) for v in mlp_grads]
        qkv_rows, mlp_grads[1:-1] = after(qkv_rows, mlp_grads[1:-1])
        qkv_pair = both_sides(hand_out(qkv_rows))
        last = len(chunks) - 1
        gate_pieces, up_pieces, down_pieces = ([(j, m * n, n) for j, (_, n) in enumerate(chunks)] for m in range(3))
        grad_w_gate, grad_w_up, grad_w_down, grad_w_o = spread(
            mlp_grads, [gate_pieces, up_pieces, down_pieces, [(last, 3 * chunks[last][1], o_n)]]
        )
        grad_w_q, grad_w_k, grad_w_v = spread([qkv_pair], [[(0, 0, q_n)], [(0, q_n, k_n)], [(0, q_n + k_n, k_n)]])
        return (
            output,
            grad_input,
            grad_w_q,
            grad_w_k,
            grad_w_v,
            grad_w_o,
            grad_w_gate,
            grad_w_up,
            grad_w_down,
            sums[:width],
            sums[width : 2 * width],
            sums[2 * width : 2 * width + head],
            sums[2 * width + head :],
        )

    return on_device


def solution(mesh):
    far = mesh.shape["shard"] // 4
    split = Mesh(mesh.devices.reshape(mesh.shape["rep"], far, 2, 2), ("rep", "far", "mid", "near"))
    tokens = P(("rep", "far", "mid", "near"), None)
    weights = P(("far", "mid", "near"), None)
    return jax.shard_map(
        build(far),
        mesh=split,
        in_specs=(tokens,) * 4 + (P(),) * 4 + (weights,) * 7,
        out_specs=(tokens,) * 2 + (weights,) * 7 + (P(),) * 4,
        check_vma=False,
    )
```
